128 devices in a mesh: gy: 8 (over z, core), gx: 16 (over x, y).
Axes of the slice: x: 4, y: 4, z: 4, core: 2. Of those that a mesh axis runs over, the one named last changes fastest.
Arguments:
- tokens_in: bfloat16 [512, 768, 256], P('gy', 'gx'), may hold values from -6 to 6
- saved_mid: bfloat16 [512, 768, 256], P('gy', 'gx'), may hold values from -6 to 6
- grad_out: bfloat16 [512, 768, 256], P('gy', 'gx'), may hold values from -6 to 6
- attn_gain: float32 [256], replicated, may hold values from 0.1 to 1.9
- mlp_gain: float32 [256], replicated, may hold values from 0.1 to 1.9
- w_query: bfloat16 [256, 256], replicated, may hold values from -1 to 1
- w_key: bfloat16 [256, 256], replicated, may hold values from -1 to 1
- w_value: bfloat16 [256, 256], replicated, may hold values from -0.375 to 0.375
- w_out: bfloat16 [256, 256], replicated, may hold values from -0.375 to 0.375
- w_up: bfloat16 [256, 1024], replicated, may hold values from -0.375 to 0.375
- conv_kernel: float32 [9, 1024], replicated, may hold values from -2 to 2
- w_down: bfloat16 [1024, 256], replicated, may hold values from -0.1875 to 0.1875
- row_mask: int32 [6, 6], replicated, may hold values from 0 to 1, as said below
- col_mask: int32 [4, 4], replicated, may hold values from 0 to 1, as said below
Outputs:
- grad_tokens: bfloat16 [512, 768, 256], P('gy', 'gx')
The draws below stay inside these ranges and needn't reach their ends.
Inputs may be any that keep to these rules, and one draw needn't show every extreme that they name: `row_mask`: every diagonal entry is 1, so each query block sees at least itself. `col_mask`: every diagonal entry is 1, so each query block sees at least itself.
All inputs are finite; a program needn't handle non-finite values.
Results may differ from the reference program's by a relative error of at most 0.04.
Values may be sent and summed in bfloat16 or wider, within the bound.
No kernel may reach another device: no remote copies, remote signals or barrier semaphores. Data moves between devices by JAX's collectives and lax.ppermute only.
A program may use at most 128 MiB of HBM per device.

```python
import jax
import jax.numpy as jnp
from jax import lax

C = 256
HEADS = 8
F = 1024
BLK = 128
TH = 64
H = 512
W = 768
NBH = 4
NBW = 6


def draw_row_mask(key, part):
    folded = jax.random.fold_in(key, 11)
    return jnp.maximum(jax.random.randint(folded, (NBW, NBW), 0, 2), jnp.eye(NBW, dtype=jnp.int32)).astype(jnp.int32)


def draw_col_mask(key, part):
    folded = jax.random.fold_in(key, 23)
    return jnp.maximum(jax.random.randint(folded, (NBH, NBH), 0, 2), jnp.eye(NBH, dtype=jnp.int32)).astype(jnp.int32)


def drawn_weight(key, salt):
    weights = jax.random.truncated_normal(jax.random.fold_in(key, salt), -6.0, 6.0, (C, C), jnp.float32) * C ** (-0.5)
    return weights.astype(jnp.bfloat16)


def draw_w_query(key, part):
    return drawn_weight(key, 41)


def draw_w_key(key, part):
    return drawn_weight(key, 43)


def draw_tokens_in(key, part):
    normal_part = jax.random.truncated_normal(jax.random.fold_in(key, 31), -6.0, 6.0, (H, W, C), jnp.float32)
    return normal_part.astype(jnp.bfloat16)


def block_scale(stream_key, dims, split, least, top_value):
    def one(dim, shards_of):
        draws = jax.random.uniform(jax.random.fold_in(jax.random.fold_in(stream_key, 6), dim), (shards_of,), jnp.float32, least / len(split), top_value / len(split))
        return jnp.repeat(jnp.exp(draws), dims[dim] // shards_of).reshape((-1,) + (1,) * (len(dims) - dim - 1))

    loudness = one(*split[0])
    for cut in split[1:]:
        loudness = loudness * one(*cut)
    return loudness


def scatter_about(own_key, dims, width, reach, split=(), kind=jnp.bfloat16):
    gain = block_scale(own_key, dims, split, -0.22, 0.18) if split else 1.0
    result = jax.random.normal(own_key, dims, jnp.float32) * width * gain
    return jnp.minimum(jnp.maximum(result, -reach), reach).astype(kind)


def setup_inputs(seed: int = 0) -> dict:
    key_of = jax.random.split(jax.random.key(seed), 15)
    tokens_in = draw_tokens_in(jax.random.fold_in(key_of[14], 71), 0)
    saved_mid = scatter_about(key_of[1], (H, W, C), 1.0, 6.0, ((0, 8), (1, 16)))
    grad_out = scatter_about(key_of[2], (H, W, C), 1.0, 6.0, ((0, 8), (1, 16)))
    attn_gain = jnp.clip(1.0 + 0.18 * jax.random.normal(key_of[3], (C,), jnp.float32), 0.1, 1.9)
    mlp_gain = jnp.clip(1.0 + 0.18 * jax.random.normal(key_of[4], (C,), jnp.float32), 0.1, 1.9)
    w_query = draw_w_query(jax.random.fold_in(key_of[14], 71), 0)
    w_key = draw_w_key(jax.random.fold_in(key_of[14], 71), 0)
    w_value = scatter_about(key_of[7], (C, C), C ** -0.5, 0.375)
    w_out = scatter_about(key_of[8], (C, C), C ** -0.5, 0.375)
    w_up = scatter_about(key_of[9], (C, F), C ** -0.5, 0.375)
    conv_kernel = scatter_about(key_of[10], (9, F), 9 ** -0.5, 2.0, (), jnp.float32)
    w_down = scatter_about(key_of[11], (F, C), F ** -0.5, 0.1875)
    row_mask = draw_row_mask(jax.random.fold_in(key_of[14], 71), 0)
    col_mask = draw_col_mask(jax.random.fold_in(key_of[14], 71), 0)
    return {"tokens_in": tokens_in, "saved_mid": saved_mid, "grad_out": grad_out, "attn_gain": attn_gain, "mlp_gain": mlp_gain, "w_query": w_query, "w_key": w_key, "w_value": w_value, "w_out": w_out, "w_up": w_up, "conv_kernel": conv_kernel, "w_down": w_down, "row_mask": row_mask, "col_mask": col_mask}


EPSILON = 1e-05
GELU_C = 0.7978845608028654

def layer_norm(values, gain_vec):
    values = values.astype(jnp.float32)
    center = values - lax.optimization_barrier(jnp.mean(values, axis=-1, keepdims=True))
    inv_std = lax.rsqrt(lax.optimization_barrier(jnp.mean(center * center, axis=-1, keepdims=True)) + EPSILON)
    normed = center * inv_std
    return (normed * gain_vec, normed, inv_std)

def norm_backward(grad_norm, gain_vec, normed, inv_std):
    grad_hat = grad_norm * gain_vec
    return inv_std * (grad_hat - lax.optimization_barrier(jnp.mean(grad_hat, axis=-1, keepdims=True)) - normed * lax.optimization_barrier(jnp.mean(grad_hat * normed, axis=-1, keepdims=True)))

def gelu_slope(value):
    inside_term = GELU_C * (value + 0.044715 * value * value * value)
    tanh_val = jnp.tanh(inside_term)
    return 0.5 * (1.0 + tanh_val) + 0.5 * value * (1.0 - tanh_val * tanh_val) * GELU_C * (1.0 + 3.0 * 0.044715 * value * value)

def mlp_band(mid_pad, grad_pad, mlp_gain, w_up, conv_kernel, w_down):
    rows_in = mid_pad.shape[0] - 4
    cols_in = mid_pad.shape[1] - 4
    mid_norm, mid_hat, mid_inv = layer_norm(mid_pad, mlp_gain)
    hidden = jnp.dot(mid_norm.astype(jnp.bfloat16), w_up, preferred_element_type=jnp.float32).astype(jnp.bfloat16)
    pre_act = jnp.zeros((rows_in + 2, cols_in + 2, hidden.shape[-1]), jnp.float32)
    for row_shift in range(3):
        for col_shift in range(3):
            pre_act = pre_act + conv_kernel[3 * row_shift + col_shift] * hidden[row_shift:row_shift + rows_in + 2, col_shift:col_shift + cols_in + 2]
    grad_act = jnp.dot(grad_pad[1:-1, 1:-1], w_down.T, preferred_element_type=jnp.float32)
    grad_pre = (grad_act * gelu_slope(pre_act)).astype(jnp.bfloat16)
    grad_hidden = jnp.zeros((rows_in, cols_in, hidden.shape[-1]), jnp.float32)
    for row_shift in range(3):
        for col_shift in range(3):
            grad_hidden = grad_hidden + conv_kernel[3 * row_shift + col_shift] * grad_pre[2 - row_shift:2 - row_shift + rows_in, 2 - col_shift:2 - col_shift + cols_in]
    grad_hidden = grad_hidden.astype(jnp.bfloat16)
    grad_norm = jnp.dot(grad_hidden, w_up.T, preferred_element_type=jnp.float32)
    norm_grad = norm_backward(grad_norm, mlp_gain, mid_hat[2:-2, 2:-2], mid_inv[2:-2, 2:-2])
    return (grad_pad[2:-2, 2:-2].astype(jnp.float32) + norm_grad).astype(jnp.bfloat16)

def block_allowed(mask_table):
    return jnp.repeat(jnp.repeat(mask_table > 0, BLK, axis=0), BLK, axis=1)

def line_grads(qkv_line, grad_line, allowed, head_count):
    length = qkv_line.shape[0]
    half_width = grad_line.shape[-1]
    head_dim = half_width // head_count
    qkv_parts = qkv_line.astype(jnp.float32).reshape(length, 3, head_count, head_dim)
    queries = qkv_parts[:, 0]
    key_heads = qkv_parts[:, 1]
    value_heads = qkv_parts[:, 2]
    grad_heads = grad_line.astype(jnp.float32).reshape(length, head_count, head_dim)
    factor = head_dim ** (-0.5)
    scores = jnp.einsum('qhd,khd->hqk', queries, key_heads) * factor
    scores = jnp.where(allowed[None], scores, -jnp.inf)
    row_top = lax.optimization_barrier(jnp.max(scores, axis=-1, keepdims=True))
    exp_terms = jnp.exp(scores - row_top)
    prob_rows = exp_terms / lax.optimization_barrier(jnp.sum(exp_terms, axis=-1, keepdims=True))
    prob_low = prob_rows.astype(jnp.bfloat16)
    attended = jnp.einsum('hqk,khd->qhd', prob_low.astype(jnp.float32), value_heads).astype(jnp.bfloat16)
    row_delta = lax.optimization_barrier(jnp.sum(grad_heads * attended.astype(jnp.float32), axis=-1))
    grad_probs = jnp.einsum('qhd,khd->hqk', grad_heads, value_heads)
    grad_scores = (prob_rows * (grad_probs - jnp.transpose(row_delta)[:, :, None])).astype(jnp.bfloat16)
    score_wide = grad_scores.astype(jnp.float32)
    grad_query = (jnp.einsum('hqk,khd->qhd', score_wide, key_heads) * factor).astype(jnp.bfloat16)
    grad_key = (jnp.einsum('hqk,qhd->khd', score_wide, queries) * factor).astype(jnp.bfloat16)
    grad_value = jnp.einsum('hqk,qhd->khd', prob_low.astype(jnp.float32), grad_heads).astype(jnp.bfloat16)
    return jnp.stack([grad_query, grad_key, grad_value], axis=1).reshape(length, 3 * half_width)

def reference(tokens_in, saved_mid, grad_out, attn_gain, mlp_gain, w_query, w_key, w_value, w_out, w_up, conv_kernel, w_down, row_mask, col_mask):
    half_width = C // 2
    pad_width = ((2, 2), (2, 2), (0, 0))
    mid_pad = jnp.pad(saved_mid, pad_width)
    grad_pad = jnp.pad(grad_out, pad_width)

    def one_band(band_index):
        row_start = (band_index * TH).astype(jnp.int32)
        mid_band = lax.dynamic_slice_in_dim(mid_pad, row_start, TH + 4, 0)
        grad_band = lax.dynamic_slice_in_dim(grad_pad, row_start, TH + 4, 0)
        return mlp_band(mid_band, grad_band, mlp_gain, w_up, conv_kernel, w_down)
    grad_mid = lax.map(one_band, jnp.arange(H // TH, dtype=jnp.int32)).reshape(H, W, C)
    grad_attn = jnp.dot(grad_mid, w_out.T, preferred_element_type=jnp.float32).astype(jnp.bfloat16)
    in_norm, in_hat, in_inv = layer_norm(tokens_in, attn_gain)
    normed_in = in_norm.astype(jnp.bfloat16)
    w_row = jnp.concatenate([w_query[:, :half_width], w_key[:, :half_width], w_value[:, :half_width]], axis=1)
    w_col = jnp.concatenate([w_query[:, half_width:], w_key[:, half_width:], w_value[:, half_width:]], axis=1)
    allowed_row = block_allowed(row_mask)
    allowed_col = block_allowed(col_mask)
    row_qkv = jnp.dot(normed_in, w_row, preferred_element_type=jnp.float32).astype(jnp.bfloat16)
    col_qkv = jnp.dot(normed_in, w_col, preferred_element_type=jnp.float32).astype(jnp.bfloat16)

    def row_line(pair_in):
        return line_grads(pair_in[0], pair_in[1], allowed_row, HEADS // 2)

    def col_line(pair_in):
        return line_grads(pair_in[0], pair_in[1], allowed_col, HEADS // 2)
    row_grads = lax.map(row_line, (row_qkv, grad_attn[..., :half_width]))
    col_grads = lax.map(col_line, (jnp.swapaxes(col_qkv, 0, 1), jnp.swapaxes(grad_attn[..., half_width:], 0, 1)))
    col_grads = jnp.swapaxes(col_grads, 0, 1)
    grad_row_in = jnp.dot(row_grads, w_row.T, preferred_element_type=jnp.float32).astype(jnp.bfloat16)
    grad_col_in = jnp.dot(col_grads, w_col.T, preferred_element_type=jnp.float32).astype(jnp.bfloat16)
    norm_grad = norm_backward(grad_row_in.astype(jnp.float32) + grad_col_in.astype(jnp.float32), attn_gain, in_hat, in_inv)
    return (grad_mid.astype(jnp.float32) + norm_grad).astype(jnp.bfloat16)
```

```python
import functools
import jax
import jax.numpy as jnp
from jax import lax
from jax.experimental import pallas as pl
from jax.experimental.pallas import tpu as pltpu
from jax.sharding import PartitionSpec as P

HEADS = 8
BLK = 128
EPSILON = 1e-05
LOG2E = 1.4426950408889634
LN2 = 0.6931471805599453
F32 = jnp.float32
BF16 = jnp.bfloat16


def attn_kernel(nl, nk, mask_ref, x_ref, g_ref, gain_ref, w_ref, wt_ref, out_ref,
                q_s, k_s, v_s, g_s, kt_s, qmt_s, qm_s, gmt_s, gm_s, e_s, dp_s, st_s, dq_s, dk_s, dv_s):
    heads = HEADS // 2
    hw = 128
    hd = hw // heads
    length = nk * BLK
    factor = hd ** -0.5
    gain = gain_ref[...]
    wide = heads * BLK

    qmt_s[...] = jnp.zeros_like(qmt_s)
    gmt_s[...] = jnp.zeros_like(gmt_s)
    dk_s[...] = jnp.zeros_like(dk_s)
    dv_s[...] = jnp.zeros_like(dv_s)

    def prepare(line, carry):
        xv = x_ref[:, line].reshape(length, 2 * hw).astype(F32)
        mean = jnp.mean(xv, axis=-1, keepdims=True)
        center = xv - mean
        inv = lax.rsqrt(jnp.mean(center * center, axis=-1, keepdims=True) + EPSILON)
        normed = (center * inv * gain).astype(BF16)
        qkv = jnp.dot(normed, w_ref[...], preferred_element_type=F32)
        kf = qkv[:, hw:2 * hw]
        q_s[line] = (qkv[:, :hw] * (factor * LOG2E)).astype(BF16)
        k_s[line] = kf.astype(BF16)
        v_s[line] = qkv[:, 2 * hw:].astype(BF16)
        kt_s[line] = kf.T.astype(BF16)
        g_s[line] = g_ref[:, line].reshape(length, hw)
        return carry

    lax.fori_loop(0, nl, prepare, 0)
    lane = lax.broadcasted_iota(jnp.int32, (BLK, hw), 1)

    def query_block(qb, carry):
        qs = pl.ds(pl.multiple_of(qb * BLK, BLK), BLK)
        for line in range(nl):
            for src, dt, dm in ((q_s, qmt_s, qm_s), (g_s, gmt_s, gm_s)):
                blk = src[line, qs, :]
                blk_f = blk.astype(F32)
                blk_t = blk_f.T.astype(BF16)
                for h in range(heads):
                    dt[line, h * hd:(h + 1) * hd, h * BLK:(h + 1) * BLK] = blk_t[h * hd:(h + 1) * hd]
                    inside = (lane >= h * hd) & (lane < (h + 1) * hd)
                    dm[line, h * BLK:(h + 1) * BLK, :] = jnp.where(inside, blk_f, 0.0).astype(BF16)

        def phase_a(kb, c):
            allowed = mask_ref[qb, kb] > 0
            ks = pl.ds(pl.multiple_of(kb * BLK, BLK), BLK)

            @pl.when(jnp.logical_not(allowed))
            def _():
                for line in range(nl):
                    st_s[kb, line] = jnp.concatenate(
                        [jnp.full((1, wide), -jnp.inf, F32), jnp.zeros((7, wide), F32)], axis=0)

            @pl.when(allowed)
            def _():
                for line in range(nl):
                    s = jnp.dot(k_s[line, ks, :], qmt_s[line], preferred_element_type=F32)
                    dp = jnp.dot(v_s[line, ks, :], gmt_s[line], preferred_element_type=F32)
                    top = jnp.max(s, axis=0, keepdims=True)
                    e = jnp.exp2(s - top)
                    e_s[kb, line] = e.astype(BF16)
                    dp_s[kb, line] = dp
                    st_s[kb, line, 0:1] = top
                    st_s[kb, line, 1:2] = jnp.sum(e, axis=0, keepdims=True)
                    st_s[kb, line, 2:3] = jnp.sum(e * dp, axis=0, keepdims=True)
            return c

        lax.fori_loop(0, nk, phase_a, 0)

        for line in range(nl):
            top = st_s[0, line, 0:1]
            for kb in range(1, nk):
                top = jnp.maximum(top, st_s[kb, line, 0:1])
            total = jnp.zeros((1, wide), F32)
            moment = jnp.zeros((1, wide), F32)
            weights = []
            for kb in range(nk):
                wk = jnp.exp2(st_s[kb, line, 0:1] - top)
                weights.append(wk)
                total = total + wk * st_s[kb, line, 1:2]
                moment = moment + wk * st_s[kb, line, 2:3]
            inv = 1.0 / total
            delta = moment * inv
            for kb in range(nk):
                st_s[kb, line, 3:4] = weights[kb] * inv
                st_s[kb, line, 4:5] = delta
            dq_s[line] = jnp.zeros((hd, wide), F32)

        def phase_b(kb, c):
            ks = pl.ds(pl.multiple_of(kb * BLK, BLK), BLK)

            @pl.when(mask_ref[qb, kb] > 0)
            def _():
                for line in range(nl):
                    p = e_s[kb, line].astype(F32) * st_s[kb, line, 3:4]
                    ds = (p * (dp_s[kb, line] - st_s[kb, line, 4:5])).astype(BF16)
                    dv_s[line, ks, :] += jnp.dot(p.astype(BF16), gm_s[line], preferred_element_type=F32)
                    dk_s[line, ks, :] += jnp.dot(ds, qm_s[line], preferred_element_type=F32)
                    for h in range(heads):
                        dq_s[line, :, h * BLK:(h + 1) * BLK] += jnp.dot(
                            kt_s[line, h * hd:(h + 1) * hd, ks], ds[:, h * BLK:(h + 1) * BLK],
                            preferred_element_type=F32)
            return c

        lax.fori_loop(0, nk, phase_b, 0)
        for line in range(nl):
            full = jnp.concatenate([dq_s[line, :, h * BLK:(h + 1) * BLK] for h in range(heads)], axis=0)
            q_s[line, qs, :] = (full.T * factor).astype(BF16)
        return carry

    lax.fori_loop(0, nk, query_block, 0)

    def finish(line, carry):
        grads = jnp.concatenate(
            [q_s[line], (dk_s[line] * LN2).astype(BF16), dv_s[line].astype(BF16)], axis=1)
        res = jnp.dot(grads, wt_ref[...], preferred_element_type=F32).astype(BF16)
        out_ref[:, line] = res.reshape(out_ref.shape[0], out_ref.shape[2], out_ref.shape[3])
        return carry

    lax.fori_loop(0, nl, finish, 0)


def attention(x, g, gain, w, mask):
    srcs, nl, span, width = x.shape
    length = srcs * span
    nk = length // BLK
    hw = width // 2
    heads = HEADS // 2
    wide = heads * BLK
    vm = pl.BlockSpec(memory_space=pltpu.VMEM)
    return pl.pallas_call(
        functools.partial(attn_kernel, nl, nk),
        out_shape=jax.ShapeDtypeStruct(x.shape, BF16),
        in_specs=[pl.BlockSpec(memory_space=pltpu.SMEM), vm, vm, vm, vm, vm],
        out_specs=vm,
        scratch_shapes=[
            pltpu.VMEM((nl, length, hw), BF16),
            pltpu.VMEM((nl, length, hw), BF16),
            pltpu.VMEM((nl, length, hw), BF16),
            pltpu.VMEM((nl, length, hw), BF16),
            pltpu.VMEM((nl, hw, length), BF16),
            pltpu.VMEM((nl, hw, wide), BF16),
            pltpu.VMEM((nl, wide, hw), BF16),
            pltpu.VMEM((nl, hw, wide), BF16),
            pltpu.VMEM((nl, wide, hw), BF16),
            pltpu.VMEM((nk, nl, BLK, wide), BF16),
            pltpu.VMEM((nk, nl, BLK, wide), F32),
            pltpu.VMEM((nk, nl, 8, wide), F32),
            pltpu.VMEM((nl, hw // heads, wide), F32),
            pltpu.VMEM((nl, length, hw), F32),
            pltpu.VMEM((nl, length, hw), F32),
        ],
        compiler_params=pltpu.CompilerParams(vmem_limit_bytes=48 * 1024 * 1024),
        name="axial_attention",
    )(mask, x, g, gain.reshape(1, -1), w, w.T)


GELU_C = 0.7978845608028654


def with_halo(shard, sides, width):
    for axis, dim in sides:
        count, length = (lax.axis_size(axis), shard.shape[dim])
        up = [(i, (i + 1) % count) for i in range(count - 1)]
        down = [(j, i) for i, j in up]
        last = lax.slice_in_dim(shard, length - width, length, axis=dim)
        initial = lax.slice_in_dim(shard, 0, width, axis=dim)
        before = lax.ppermute(last, axis, up)
        after = lax.ppermute(initial, axis, down)
        shard = jnp.concatenate([before, shard, after], axis=dim)
    return shard


def layer_norm(values, gain_vec):
    values = values.astype(jnp.float32)
    center = values - jnp.mean(values, axis=-1, keepdims=True)
    inv_std = lax.rsqrt(jnp.mean(center * center, axis=-1, keepdims=True) + EPSILON)
    normed = center * inv_std
    return (normed * gain_vec, normed, inv_std)


def norm_backward(grad_norm, gain_vec, normed, inv_std):
    grad_hat = grad_norm * gain_vec
    return inv_std * (
        grad_hat
        - jnp.mean(grad_hat, axis=-1, keepdims=True)
        - normed * jnp.mean(grad_hat * normed, axis=-1, keepdims=True)
    )


def gelu_slope(value):
    inside_term = GELU_C * (value + 0.044715 * value * value * value)
    tanh_val = jnp.tanh(inside_term)
    return 0.5 * (1.0 + tanh_val) + 0.5 * value * (1.0 - tanh_val * tanh_val) * GELU_C * (
        1.0 + 3.0 * 0.044715 * value * value
    )


def mlp_band(mid_pad, grad_pad, mlp_gain, w_up, conv_kernel, w_down):
    rows_in = mid_pad.shape[0] - 4
    cols_in = mid_pad.shape[1] - 4
    mid_norm, mid_hat, mid_inv = layer_norm(mid_pad, mlp_gain)
    hidden = jnp.dot(
        mid_norm.astype(jnp.bfloat16), w_up, preferred_element_type=jnp.float32
    ).astype(jnp.bfloat16)
    pre_act = jnp.zeros((rows_in + 2, cols_in + 2, hidden.shape[-1]), jnp.float32)
    for row_shift in range(3):
        for col_shift in range(3):
            pre_act = (
                pre_act
                + conv_kernel[3 * row_shift + col_shift]
                * hidden[row_shift : row_shift + rows_in + 2, col_shift : col_shift + cols_in + 2]
            )
    grad_act = jnp.dot(grad_pad[1:-1, 1:-1], w_down.T, preferred_element_type=jnp.float32)
    grad_pre = (grad_act * gelu_slope(pre_act)).astype(jnp.bfloat16)
    grad_hidden = jnp.zeros((rows_in, cols_in, hidden.shape[-1]), jnp.float32)
    for row_shift in range(3):
        for col_shift in range(3):
            grad_hidden = (
                grad_hidden
                + conv_kernel[3 * row_shift + col_shift]
                * grad_pre[
                    2 - row_shift : 2 - row_shift + rows_in, 2 - col_shift : 2 - col_shift + cols_in
                ]
            )
    grad_hidden = grad_hidden.astype(jnp.bfloat16)
    grad_norm = jnp.dot(grad_hidden, w_up.T, preferred_element_type=jnp.float32)
    norm_grad = norm_backward(grad_norm, mlp_gain, mid_hat[2:-2, 2:-2], mid_inv[2:-2, 2:-2])
    return (grad_pad[2:-2, 2:-2].astype(jnp.float32) + norm_grad).astype(jnp.bfloat16)


def to_lines(blocks, axis):
    return lax.all_to_all(blocks, axis, split_axis=0, concat_axis=0, tiled=True)


def cut_cols(tile, count):
    rows, cols, width = tile.shape
    return jnp.transpose(tile.reshape(rows, count, cols // count, width), (1, 2, 0, 3))


def per_device(
    tokens_in,
    saved_mid,
    grad_out,
    attn_gain,
    mlp_gain,
    w_query,
    w_key,
    w_value,
    w_out,
    w_up,
    conv_kernel,
    w_down,
    row_mask,
    col_mask,
):
    model_width = tokens_in.shape[-1]
    half_width = model_width // 2
    tile_rows = tokens_in.shape[0]
    tile_cols = tokens_in.shape[1]
    count_gx = lax.axis_size("gx")
    count_gy = lax.axis_size("gy")
    joined = jnp.concatenate([saved_mid, grad_out], axis=-1)
    padded = with_halo(joined, (("gy", 0), ("gx", 1)), 2)
    grad_mid = mlp_band(
        padded[..., :model_width], padded[..., model_width:], mlp_gain, w_up, conv_kernel, w_down
    )
    grad_attn = jnp.dot(grad_mid, w_out.T, preferred_element_type=jnp.float32).astype(jnp.bfloat16)
    in_norm, in_hat, in_inv = layer_norm(tokens_in, attn_gain)
    w_row = jnp.concatenate(
        [w_query[:, :half_width], w_key[:, :half_width], w_value[:, :half_width]], axis=1
    )
    w_col = jnp.concatenate(
        [w_query[:, half_width:], w_key[:, half_width:], w_value[:, half_width:]], axis=1
    )
    row_shape = (count_gx, tile_rows // count_gx, tile_cols)
    row_tokens = to_lines(tokens_in.reshape(*row_shape, model_width), "gx")
    row_grads = to_lines(grad_attn[..., :half_width].reshape(*row_shape, half_width), "gx")
    col_tokens = to_lines(cut_cols(tokens_in, count_gy), "gy")
    col_grads = to_lines(cut_cols(grad_attn[..., half_width:], count_gy), "gy")
    row_out = attention(row_tokens, row_grads, attn_gain, w_row, row_mask)
    grad_row_in = to_lines(row_out, "gx").reshape(tile_rows, tile_cols, model_width)
    col_out = attention(col_tokens, col_grads, attn_gain, w_col, col_mask)
    col_back = to_lines(col_out, "gy")
    grad_col_in = jnp.transpose(col_back, (2, 0, 1, 3)).reshape(tile_rows, tile_cols, model_width)
    norm_grad = norm_backward(
        grad_row_in.astype(jnp.float32) + grad_col_in.astype(jnp.float32), attn_gain, in_hat, in_inv
    )
    return (grad_mid.astype(jnp.float32) + norm_grad).astype(jnp.bfloat16)


def solution(mesh):
    in_specs = (
        P("gy", "gx", None),
        P("gy", "gx", None),
        P("gy", "gx", None),
        P(),
        P(),
        P(),
        P(),
        P(),
        P(),
        P(),
        P(),
        P(),
        P(),
        P(),
    )
    out_specs = P("gy", "gx", None)
    return jax.shard_map(
        per_device, mesh=mesh, in_specs=in_specs, out_specs=out_specs, check_vma=False
    )
```

```python
import functools

import jax
import jax.numpy as jnp
from jax import lax
from jax.experimental import pallas as pl
from jax.experimental.pallas import tpu as pltpu
from jax.sharding import PartitionSpec as P

HEADS = 8
BLK = 128
EPSILON = 1e-05
GELU_C = 0.7978845608028654
LOG2E = 1.4426950408889634
LN2 = 0.6931471805599453
F32 = jnp.float32
BF16 = jnp.bfloat16
STRIDE = 64
GROUP = 4
CHUNK = GROUP * STRIDE
BIG = 8
GUARD = 2 * GROUP + 4
FC = 256


def dot_nt(a, b):
    return lax.dot_general(a, b, (((1,), (1,)), ((), ())), preferred_element_type=F32)


def gelu_slope(v):
    k = lambda x: jnp.asarray(x, v.dtype)
    u = v * v
    t = jnp.tanh(v * (k(GELU_C) + k(GELU_C * 0.044715) * u))
    poly = v * (k(0.5 * GELU_C) + k(1.5 * 0.044715 * GELU_C) * u)
    return (k(0.5) + k(0.5) * t) + (k(1.0) - t * t) * poly


def normalize(x):
    center = x - jnp.mean(x, axis=-1, keepdims=True)
    inv = lax.rsqrt(jnp.mean(center * center, axis=-1, keepdims=True) + EPSILON)
    return center * inv, inv


def mlp_kernel(rows, cols, mid_ref, gout_ref, rowh_ref, edge_ref, gain_ref, wup_ref, conv_ref, wdown_ref, wout_ref,
               gm_ref, grow_ref, gcol_ref, x_s, h_s, gp_s, y_s, wdt_s, wut_s, grad_s):
    step = pl.program_id(0)
    width = mid_ref.shape[-1]
    gain = gain_ref[...]
    held = rows + 8
    trips = (rows + 4 + GROUP) // GROUP + 2
    tall = BIG * STRIDE

    def rows_at(row):
        return pl.multiple_of(row * STRIDE, STRIDE)

    @pl.when(step == 0)
    def _():
        edges = STRIDE - cols

        def place(ref, lead, row, values, count):
            for j in range(values.shape[0] // count):
                start = (row + j) * STRIDE + (0 if count == cols else cols)
                ref[lead + (pl.ds(pl.multiple_of(start, 16), count), slice(None))] = values[j * count:(j + 1) * count]

        def scaled(values):
            return normalize(values.astype(F32))[0] * gain

        none = jnp.zeros((cols, width), F32)
        for row in (0, 1, rows + 6, rows + 7, rows + 8, rows + 9):
            place(y_s, (0,), row, none, cols)
            place(grad_s, (), row, none.astype(BF16), cols)
        halo = rowh_ref[...].reshape(4 * cols, 2 * width)
        for part, row in ((0, 2), (1, rows + 4)):
            values = halo[part * 2 * cols:(part + 1) * 2 * cols]
            place(y_s, (0,), row, scaled(values[:, :width]), cols)
            place(grad_s, (), row, values[:, width:], cols)

        def edge_block(i, c):
            n = (rows + 10) // 2
            values = edge_ref[pl.ds(i * n, n)].reshape(n * edges, 2 * width)
            place(y_s, (0,), i * n, scaled(values[:, :width]), edges)
            place(grad_s, (), i * n, values[:, width:], edges)
            return c
        lax.fori_loop(0, 2, edge_block, 0)

        def norm_block(i, c):
            src = pl.ds(i * BIG, BIG)
            place(y_s, (0,), i * BIG + 4, scaled(mid_ref[src].reshape(BIG * cols, width)), cols)
            place(grad_s, (), i * BIG + 4, gout_ref[src].reshape(BIG * cols, width), cols)
            return c
        lax.fori_loop(0, rows // BIG, norm_block, 0)

        def shift_block(i, c):
            at = rows_at(i * BIG + 1)
            xv = y_s[0, pl.ds(at, tall + 8), :]
            lv = y_s[0, pl.ds(at - 8, tall + 8), :]
            dst = pl.ds(rows_at(i * BIG), tall)
            x_s[0, dst, :] = lv[7:7 + tall].astype(BF16)
            x_s[1, dst, :] = xv[:tall].astype(BF16)
            x_s[2, dst, :] = xv[1:1 + tall].astype(BF16)
            return c
        lax.fori_loop(0, held // BIG, shift_block, 0)

    wdt_s[...] = wdown_ref[...].astype(F32).T.astype(BF16)
    wut_s[...] = wup_ref[...].astype(F32).T.astype(BF16)
    taps = [conv_ref[t:t + 1, :].astype(BF16) for t in range(9)]
    first = step == 0

    def body(i, c):
        z0 = GROUP * (i - 2) - 2 + GUARD
        for b in range(3):
            parts = []
            for sub in range(GROUP):
                z = None
                for a in range(3):
                    term = gp_s[pl.ds(rows_at(z0 + 1 - a + sub), STRIDE), :] * taps[3 * a + b]
                    z = term if z is None else z + term
                parts.append(z)
            old = y_s[b, pl.ds(rows_at(z0), CHUNK), :]
            y_s[b, pl.ds(rows_at(z0), CHUNK), :] = jnp.where(first, 0.0, old) + jnp.dot(
                jnp.concatenate(parts, axis=0), wut_s[...], preferred_element_type=F32)
        g0 = GROUP * (i - 1) - 1
        ga = jnp.dot(grad_s[pl.ds(rows_at(jnp.clip(g0 + 1, 0, held + 2 - GROUP)), CHUNK), :], wdt_s[...],
                     preferred_element_type=F32)
        for sub in range(GROUP):
            pre = None
            for a in range(3):
                for b in range(3):
                    term = h_s[b, pl.ds(rows_at(g0 + GUARD + a - 1 + sub), STRIDE), :] * taps[3 * a + b]
                    pre = term if pre is None else pre + term
            gp_s[pl.ds(rows_at(g0 + GUARD + sub), STRIDE), :] = (
                ga[sub * STRIDE:(sub + 1) * STRIDE] * gelu_slope(pre).astype(F32)).astype(BF16)
        src = pl.ds(rows_at(jnp.minimum(GROUP * i, held - GROUP)), CHUNK)
        for b in range(3):
            h_s[b, pl.ds(rows_at(GROUP * i + GUARD), CHUNK), :] = jnp.dot(
                x_s[b, src, :], wup_ref[...], preferred_element_type=F32).astype(BF16)
        return c

    lax.fori_loop(0, trips, body, 0)

    @pl.when(step == pl.num_programs(0) - 1)
    def _():
        def finish(i, c):
            base = rows_at(i * BIG + 3 + GUARD)
            right = y_s[0, pl.ds(base, tall + 8), :][1:1 + tall]
            left = y_s[2, pl.ds(base - 8, tall + 8), :][7:7 + tall]
            total = y_s[1, pl.ds(base, tall), :] + right + left

            def crop(v):
                return v.reshape(BIG, STRIDE, width)[:, :cols].reshape(BIG * cols, width)

            e = crop(total) * gain
            src = pl.ds(i * BIG, BIG)
            hat, inv = normalize(mid_ref[src].reshape(BIG * cols, width).astype(F32))
            res = gout_ref[src].reshape(BIG * cols, width).astype(F32) + inv * (
                e - jnp.mean(e, axis=-1, keepdims=True) - hat * jnp.mean(e * hat, axis=-1, keepdims=True))
            res = res.astype(BF16)
            dst = pl.ds(i * BIG, BIG)
            gm_ref[dst] = res.reshape(BIG, cols, width)
            ga = dot_nt(res, wout_ref[...]).astype(BF16)
            grow_ref[dst] = ga[:, :width // 2].reshape(BIG, cols, width // 2)
            gcol_ref[dst] = ga[:, width // 2:].reshape(BIG, cols, width // 2)
            return c
        lax.fori_loop(0, rows // BIG, finish, 0)


def mlp(mid, grad, halo, edge, gain, w_up, conv_kernel, w_down, w_out):
    rows, cols, width = mid.shape
    hidden = w_up.shape[1]
    held = rows + 8
    trips = (rows + 4 + GROUP) // GROUP + 2
    slots = (GROUP * trips + GUARD + 1) * STRIDE
    whole = pl.BlockSpec(memory_space=pltpu.VMEM)
    half = jax.ShapeDtypeStruct((rows, cols, width // 2), BF16)
    return pl.pallas_call(
        functools.partial(mlp_kernel, rows, cols),
        out_shape=(jax.ShapeDtypeStruct((rows, cols, width), BF16), half, half),
        grid=(hidden // FC,),
        in_specs=[whole, whole, whole, whole, whole,
                  pl.BlockSpec((width, FC), lambda i: (0, i)),
                  pl.BlockSpec((9, FC), lambda i: (0, i)),
                  pl.BlockSpec((FC, width), lambda i: (i, 0)),
                  whole],
        out_specs=(whole, whole, whole),
        scratch_shapes=[
            pltpu.VMEM((3, held * STRIDE, width), BF16),
            pltpu.VMEM((3, slots, FC), BF16),
            pltpu.VMEM((slots, FC), BF16),
            pltpu.VMEM((3, slots, width), F32),
            pltpu.VMEM((width, FC), BF16),
            pltpu.VMEM((FC, width), BF16),
            pltpu.VMEM(((rows + 10) * STRIDE, width), BF16),
        ],
        compiler_params=pltpu.CompilerParams(vmem_limit_bytes=60 * 1024 * 1024),
        cost_estimate=pl.CostEstimate(flops=20_000_000_000, transcendentals=4_000_000, bytes_accessed=12_000_000),
        name="mlp_backward",
    )(mid, grad, halo, edge, gain.reshape(1, -1), w_up, conv_kernel, w_down, w_out)


def attn_kernel(nl, nk, half, split, mask_ref, *refs):
    (x_ref, g_ref, gain_ref, wq_ref, wk_ref, wv_ref, out_ref, w_s, wt_s,
     q_s, k_s, v_s, g_s, kt_s, qmt_s, qm_s, gmt_s, gm_s, e_s, dp_s, st_s, dq_s, dk_s, dv_s) = refs if not split else refs[:1] + refs[:1] + refs[1:]
    heads = HEADS // 2
    hw = 128
    hd = hw // heads
    length = nk * BLK
    factor = hd ** -0.5
    gain = gain_ref[...]
    wide = heads * BLK

    qmt_s[...] = jnp.zeros_like(qmt_s)
    gmt_s[...] = jnp.zeros_like(gmt_s)
    dk_s[...] = jnp.zeros_like(dk_s)
    dv_s[...] = jnp.zeros_like(dv_s)

    for j, ref in enumerate((wq_ref, wk_ref, wv_ref)):
        part = ref[:, half * hw:(half + 1) * hw]
        w_s[:, j * hw:(j + 1) * hw] = part
        wt_s[j * hw:(j + 1) * hw, :] = part.astype(F32).T.astype(BF16)

    def prepare(line, carry):
        xv = (x_ref[:, line, :, :2 * hw] if split else x_ref[:, line]).reshape(length, 2 * hw).astype(F32)
        mean = jnp.mean(xv, axis=-1, keepdims=True)
        center = xv - mean
        inv = lax.rsqrt(jnp.mean(center * center, axis=-1, keepdims=True) + EPSILON)
        normed = (center * inv * gain).astype(BF16)
        qkv = jnp.dot(normed, w_s[...], preferred_element_type=F32)
        kf = qkv[:, hw:2 * hw]
        q_s[line] = (qkv[:, :hw] * (factor * LOG2E)).astype(BF16)
        k_s[line] = kf.astype(BF16)
        v_s[line] = qkv[:, 2 * hw:].astype(BF16)
        kt_s[line] = kf.T.astype(BF16)
        g_s[line] = (g_ref[:, line, :, 2 * hw:] if split else g_ref[:, line]).reshape(length, hw)
        return carry

    lax.fori_loop(0, nl, prepare, 0)
    lane = lax.broadcasted_iota(jnp.int32, (BLK, hw), 1)

    def query_block(qb, carry):
        qs = pl.ds(pl.multiple_of(qb * BLK, BLK), BLK)
        for line in range(nl):
            for src, dt, dm in ((q_s, qmt_s, qm_s), (g_s, gmt_s, gm_s)):
                blk = src[line, qs, :]
                blk_f = blk.astype(F32)
                blk_t = blk_f.T.astype(BF16)
                for h in range(heads):
                    dt[line, h * hd:(h + 1) * hd, h * BLK:(h + 1) * BLK] = blk_t[h * hd:(h + 1) * hd]
                    inside = (lane >= h * hd) & (lane < (h + 1) * hd)
                    dm[line, h * BLK:(h + 1) * BLK, :] = jnp.where(inside, blk_f, 0.0).astype(BF16)

        def phase_a(kb, c):
            allowed = mask_ref[qb, kb] > 0
            ks = pl.ds(pl.multiple_of(kb * BLK, BLK), BLK)

            @pl.when(jnp.logical_not(allowed))
            def _():
                for line in range(nl):
                    st_s[kb, line] = jnp.concatenate(
                        [jnp.full((1, wide), -jnp.inf, F32), jnp.zeros((7, wide), F32)], axis=0)

            @pl.when(allowed)
            def _():
                for line in range(nl):
                    s = jnp.dot(k_s[line, ks, :], qmt_s[line], preferred_element_type=F32)
                    dp = jnp.dot(v_s[line, ks, :], gmt_s[line], preferred_element_type=F32)
                    top = jnp.max(s, axis=0, keepdims=True)
                    e = jnp.exp2(s - top)
                    e_s[kb, line] = e.astype(BF16)
                    dp_s[kb, line] = dp
                    st_s[kb, line, 0:1] = top
                    st_s[kb, line, 1:2] = jnp.sum(e, axis=0, keepdims=True)
                    st_s[kb, line, 2:3] = jnp.sum(e * dp, axis=0, keepdims=True)
            return c

        lax.fori_loop(0, nk, phase_a, 0)

        for line in range(nl):
            top = st_s[0, line, 0:1]
            for kb in range(1, nk):
                top = jnp.maximum(top, st_s[kb, line, 0:1])
            total = jnp.zeros((1, wide), F32)
            moment = jnp.zeros((1, wide), F32)
            weights = []
            for kb in range(nk):
                wk = jnp.exp2(st_s[kb, line, 0:1] - top)
                weights.append(wk)
                total = total + wk * st_s[kb, line, 1:2]
                moment = moment + wk * st_s[kb, line, 2:3]
            inv = 1.0 / total
            delta = moment * inv
            for kb in range(nk):
                st_s[kb, line, 3:4] = weights[kb] * inv
                st_s[kb, line, 4:5] = delta
            dq_s[line] = jnp.zeros((hd, wide), F32)

        def phase_b(kb, c):
            ks = pl.ds(pl.multiple_of(kb * BLK, BLK), BLK)

            @pl.when(mask_ref[qb, kb] > 0)
            def _():
                for line in range(nl):
                    p = e_s[kb, line].astype(F32) * st_s[kb, line, 3:4]
                    ds = (p * (dp_s[kb, line] - st_s[kb, line, 4:5])).astype(BF16)
                    dv_s[line, ks, :] += jnp.dot(p.astype(BF16), gm_s[line], preferred_element_type=F32)
                    dk_s[line, ks, :] += jnp.dot(ds, qm_s[line], preferred_element_type=F32)
                    for h in range(heads):
                        dq_s[line, :, h * BLK:(h + 1) * BLK] += jnp.dot(
                            kt_s[line, h * hd:(h + 1) * hd, ks], ds[:, h * BLK:(h + 1) * BLK],
                            preferred_element_type=F32)
            return c

        lax.fori_loop(0, nk, phase_b, 0)
        for line in range(nl):
            full = jnp.concatenate([dq_s[line, :, h * BLK:(h + 1) * BLK] for h in range(heads)], axis=0)
            q_s[line, qs, :] = (full.T * factor).astype(BF16)
        return carry

    lax.fori_loop(0, nk, query_block, 0)

    def finish(line, carry):
        grads = jnp.concatenate(
            [q_s[line], (dk_s[line] * LN2).astype(BF16), dv_s[line].astype(BF16)], axis=1)
        res = jnp.dot(grads, wt_s[...], preferred_element_type=F32).astype(BF16)
        out_ref[:, line] = res.reshape(out_ref.shape[0], out_ref.shape[2], out_ref.shape[3])
        return carry

    lax.fori_loop(0, nl, finish, 0)


def attention(arrays, gain, w_query, w_key, w_value, mask, half):
    srcs, nl, span = arrays[0].shape[:3]
    width = w_query.shape[0]
    length = srcs * span
    nk = length // BLK
    hw = width // 2
    heads = HEADS // 2
    wide = heads * BLK
    vm = pl.BlockSpec(memory_space=pltpu.VMEM)
    pairs = nk * nk * nl
    return pl.pallas_call(
        functools.partial(attn_kernel, nl, nk, half, len(arrays) == 1),
        out_shape=jax.ShapeDtypeStruct((srcs, nl, span, width), BF16),
        in_specs=[pl.BlockSpec(memory_space=pltpu.SMEM)] + [vm] * (len(arrays) + 4),
        out_specs=vm,
        scratch_shapes=[
            pltpu.VMEM((width, 3 * hw), BF16),
            pltpu.VMEM((3 * hw, width), BF16),
            pltpu.VMEM((nl, length, hw), BF16),
            pltpu.VMEM((nl, length, hw), BF16),
            pltpu.VMEM((nl, length, hw), BF16),
            pltpu.VMEM((nl, length, hw), BF16),
            pltpu.VMEM((nl, hw, length), BF16),
            pltpu.VMEM((nl, hw, wide), BF16),
            pltpu.VMEM((nl, wide, hw), BF16),
            pltpu.VMEM((nl, hw, wide), BF16),
            pltpu.VMEM((nl, wide, hw), BF16),
            pltpu.VMEM((nk, nl, BLK, wide), BF16),
            pltpu.VMEM((nk, nl, BLK, wide), F32),
            pltpu.VMEM((nk, nl, 8, wide), F32),
            pltpu.VMEM((nl, hw // heads, wide), F32),
            pltpu.VMEM((nl, length, hw), F32),
            pltpu.VMEM((nl, length, hw), F32),
        ],
        compiler_params=pltpu.CompilerParams(vmem_limit_bytes=40 * 1024 * 1024),
        cost_estimate=pl.CostEstimate(flops=pairs * 200_000_000, transcendentals=pairs * 65536, bytes_accessed=4_000_000),
        name="axial_attention",
    )(mask, *arrays, gain.reshape(1, -1), w_query, w_key, w_value)


def final_kernel(tok_ref, mid_ref, row_ref, col_ref, gain_ref, out_ref):
    count, cols, width = tok_ref.shape

    def flat(ref):
        return ref[...].reshape(count * cols, width).astype(F32)

    hat, inv = normalize(flat(tok_ref))
    e = (flat(row_ref) + flat(col_ref)) * gain_ref[...]
    res = flat(mid_ref) + inv * (
        e - jnp.mean(e, axis=-1, keepdims=True) - hat * jnp.mean(e * hat, axis=-1, keepdims=True))
    out_ref[...] = res.astype(BF16).reshape(count, cols, width)


def final(tokens, grad_mid, row_back, col_back, gain):
    rows, cols, width = tokens.shape
    blk = pl.BlockSpec((8, cols, width), lambda i: (i, 0, 0))
    return pl.pallas_call(
        final_kernel,
        out_shape=jax.ShapeDtypeStruct(tokens.shape, BF16),
        grid=(rows // 8,),
        in_specs=[blk, blk, blk, blk, pl.BlockSpec((1, width), lambda i: (0, 0))],
        out_specs=blk,
        cost_estimate=pl.CostEstimate(flops=20_000_000, transcendentals=4_000, bytes_accessed=8_000_000),
        name="norm_backward",
    )(tokens, grad_mid, row_back, col_back, gain.reshape(1, -1))


def to_lines(blocks, axis):
    return lax.all_to_all(blocks, axis, split_axis=0, concat_axis=0, tiled=True)


def cut_cols(tile, count):
    rows, cols, width = tile.shape
    return jnp.transpose(tile.reshape(rows, count, cols // count, width), (1, 2, 0, 3))


def neighbours(ahead, behind, axis):
    count = lax.axis_size(axis)
    up = [(i, i + 1) for i in range(count - 1)]
    return lax.ppermute(ahead, axis, up), lax.ppermute(behind, axis, [(j, i) for i, j in up])


def per_device(tokens_in, saved_mid, grad_out, attn_gain, mlp_gain, w_query, w_key, w_value, w_out,
               w_up, conv_kernel, w_down, row_mask, col_mask):
    rows, cols, width = tokens_in.shape
    half = width // 2
    count_gx = lax.axis_size("gx")
    count_gy = lax.axis_size("gy")

    def both(rs, cs):
        return jnp.concatenate([saved_mid[rs, cs], grad_out[rs, cs]], axis=-1)

    every = slice(None)
    above, below = neighbours(both(slice(rows - 2, rows), every), both(slice(0, 2), every), "gy")
    row_tokens = to_lines(tokens_in.reshape(count_gx, rows // count_gx, cols, width), "gx")
    sides = [jnp.concatenate([above[:, cs], both(every, cs), below[:, cs]], axis=0)
             for cs in (slice(cols - 2, cols), slice(0, 2))]
    left, right = neighbours(sides[0], sides[1], "gx")
    edge = jnp.concatenate([
        jnp.pad(right, ((2, 4), (0, 0), (0, 0))),
        jnp.zeros((rows + 10, STRIDE - cols - 4, 2 * width), BF16),
        jnp.pad(left, ((1, 5), (0, 0), (0, 0)))], axis=1)
    halo = jnp.concatenate([above, below], axis=0)
    grad_mid, grad_row, grad_col = mlp(
        saved_mid, grad_out, halo, edge, mlp_gain, w_up, conv_kernel, w_down, w_out)
    grad_row = to_lines(grad_row.reshape(count_gx, rows // count_gx, cols, half), "gx")
    col_lines = to_lines(cut_cols(jnp.concatenate([tokens_in, grad_col], axis=-1), count_gy), "gy")
    weights = (w_query, w_key, w_value)
    row_out = attention((row_tokens, grad_row), attn_gain, *weights, row_mask, 0)
    row_back = to_lines(row_out, "gx").reshape(rows, cols, width)
    col_out = attention((col_lines,), attn_gain, *weights, col_mask, 1)
    col_back = jnp.transpose(to_lines(col_out, "gy"), (2, 0, 1, 3)).reshape(rows, cols, width)
    return final(tokens_in, grad_mid, row_back, col_back, attn_gain)


def solution(mesh):
    tile = P("gy", "gx", None)
    return jax.shard_map(per_device, mesh=mesh, in_specs=(tile,) * 3 + (P(),) * 11, out_specs=tile, check_vma=False)
```

```python
import functools

import jax
import jax.numpy as jnp
from jax import lax
from jax.experimental import pallas as pl
from jax.experimental.pallas import tpu as pltpu
from jax.sharding import PartitionSpec as P

HEADS = 8
BLK = 128
EPSILON = 1e-05
GELU_C = 0.7978845608028654
LOG2E = 1.4426950408889634
LN2 = 0.6931471805599453
F32 = jnp.float32
BF16 = jnp.bfloat16
STRIDE = 64
GROUP = 4
CHUNK = GROUP * STRIDE
BIG = 8
GUARD = 2 * GROUP + 4
FC = 256


def dot_nt(a, b):
    return lax.dot_general(a, b, (((1,), (1,)), ((), ())), preferred_element_type=F32)


def gelu_slope(v):
    k = lambda x: jnp.asarray(x, v.dtype)
    u = v * v
    t = jnp.tanh(v * (k(GELU_C) + k(GELU_C * 0.044715) * u))
    poly = v * (k(0.5 * GELU_C) + k(1.5 * 0.044715 * GELU_C) * u)
    return (k(0.5) + k(0.5) * t) + (k(1.0) - t * t) * poly


def normalize(x):
    center = x - jnp.mean(x, axis=-1, keepdims=True)
    inv = lax.rsqrt(jnp.mean(center * center, axis=-1, keepdims=True) + EPSILON)
    return center * inv, inv


def mlp_kernel(rows, cols, mid_ref, gout_ref, rowh_ref, edge_ref, gain_ref, wup_ref, conv_ref, wdown_ref, wout_ref,
               gm_ref, grow_ref, gcol_ref, x_s, h_s, gp_s, y_s, wdt_s, wut_s, grad_s):
    step = pl.program_id(0)
    width = mid_ref.shape[-1]
    gain = gain_ref[...]
    held = rows + 8
    trips = (rows + 4 + GROUP) // GROUP + 2
    tall = BIG * STRIDE

    def rows_at(row):
        return pl.multiple_of(row * STRIDE, STRIDE)

    @pl.when(step == 0)
    def _():
        edges = STRIDE - cols

        def place(ref, lead, row, values, count):
            for j in range(values.shape[0] // count):
                start = (row + j) * STRIDE + (0 if count == cols else cols)
                ref[lead + (pl.ds(pl.multiple_of(start, 16), count), slice(None))] = values[j * count:(j + 1) * count]

        def scaled(values):
            return normalize(values.astype(F32))[0] * gain

        none = jnp.zeros((cols, width), F32)
        for row in (0, 1, rows + 6, rows + 7, rows + 8, rows + 9):
            place(y_s, (0,), row, none, cols)
            place(grad_s, (), row, none.astype(BF16), cols)
        halo = rowh_ref[...].reshape(4 * cols, 2 * width)
        for part, row in ((0, 2), (1, rows + 4)):
            values = halo[part * 2 * cols:(part + 1) * 2 * cols]
            place(y_s, (0,), row, scaled(values[:, :width]), cols)
            place(grad_s, (), row, values[:, width:], cols)

        def edge_block(i, c):
            n = (rows + 10) // 2
            values = edge_ref[pl.ds(i * n, n)].reshape(n * edges, 2 * width)
            place(y_s, (0,), i * n, scaled(values[:, :width]), edges)
            place(grad_s, (), i * n, values[:, width:], edges)
            return c
        lax.fori_loop(0, 2, edge_block, 0)

        def norm_block(i, c):
            src = pl.ds(i * BIG, BIG)
            place(y_s, (0,), i * BIG + 4, scaled(mid_ref[src].reshape(BIG * cols, width)), cols)
            place(grad_s, (), i * BIG + 4, gout_ref[src].reshape(BIG * cols, width), cols)
            return c
        lax.fori_loop(0, rows // BIG, norm_block, 0)

        def shift_block(i, c):
            at = rows_at(i * BIG + 1)
            xv = y_s[0, pl.ds(at, tall + 8), :]
            lv = y_s[0, pl.ds(at - 8, tall + 8), :]
            dst = pl.ds(rows_at(i * BIG), tall)
            x_s[0, dst, :] = lv[7:7 + tall].astype(BF16)
            x_s[1, dst, :] = xv[:tall].astype(BF16)
            x_s[2, dst, :] = xv[1:1 + tall].astype(BF16)
            return c
        lax.fori_loop(0, held // BIG, shift_block, 0)

    wdt_s[...] = wdown_ref[...].astype(F32).T.astype(BF16)
    wut_s[...] = wup_ref[...].astype(F32).T.astype(BF16)
    taps = [conv_ref[t:t + 1, :].astype(BF16) for t in range(9)]
    first = step == 0

    def body(i, c):
        z0 = GROUP * (i - 2) - 2 + GUARD
        for b in range(3):
            parts = []
            for sub in range(GROUP):
                z = None
                for a in range(3):
                    term = gp_s[pl.ds(rows_at(z0 + 1 - a + sub), STRIDE), :] * taps[3 * a + b]
                    z = term if z is None else z + term
                parts.append(z)
            old = y_s[b, pl.ds(rows_at(z0), CHUNK), :]
            y_s[b, pl.ds(rows_at(z0), CHUNK), :] = jnp.where(first, 0.0, old) + jnp.dot(
                jnp.concatenate(parts, axis=0), wut_s[...], preferred_element_type=F32)
        g0 = GROUP * (i - 1) - 1
        ga = jnp.dot(grad_s[pl.ds(rows_at(jnp.clip(g0 + 1, 0, held + 2 - GROUP)), CHUNK), :], wdt_s[...],
                     preferred_element_type=F32)
        for sub in range(GROUP):
            pre = None
            for a in range(3):
                for b in range(3):
                    term = h_s[b, pl.ds(rows_at(g0 + GUARD + a - 1 + sub), STRIDE), :] * taps[3 * a + b]
                    pre = term if pre is None else pre + term
            gp_s[pl.ds(rows_at(g0 + GUARD + sub), STRIDE), :] = (
                ga[sub * STRIDE:(sub + 1) * STRIDE] * gelu_slope(pre).astype(F32)).astype(BF16)
        src = pl.ds(rows_at(jnp.minimum(GROUP * i, held - GROUP)), CHUNK)
        for b in range(3):
            h_s[b, pl.ds(rows_at(GROUP * i + GUARD), CHUNK), :] = jnp.dot(
                x_s[b, src, :], wup_ref[...], preferred_element_type=F32).astype(BF16)
        return c

    lax.fori_loop(0, trips, body, 0)

    @pl.when(step == pl.num_programs(0) - 1)
    def _():
        def finish(i, c):
            base = rows_at(i * BIG + 3 + GUARD)
            right = y_s[0, pl.ds(base, tall + 8), :][1:1 + tall]
            left = y_s[2, pl.ds(base - 8, tall + 8), :][7:7 + tall]
            total = y_s[1, pl.ds(base, tall), :] + right + left

            def crop(v):
                return v.reshape(BIG, STRIDE, width)[:, :cols].reshape(BIG * cols, width)

            e = crop(total) * gain
            src = pl.ds(i * BIG, BIG)
            hat, inv = normalize(mid_ref[src].reshape(BIG * cols, width).astype(F32))
            res = gout_ref[src].reshape(BIG * cols, width).astype(F32) + inv * (
                e - jnp.mean(e, axis=-1, keepdims=True) - hat * jnp.mean(e * hat, axis=-1, keepdims=True))
            res = res.astype(BF16)
            dst = pl.ds(i * BIG, BIG)
            gm_ref[dst] = res.reshape(BIG, cols, width)
            ga = dot_nt(res, wout_ref[...]).astype(BF16)
            grow_ref[dst] = ga[:, :width // 2].reshape(BIG, cols, width // 2)
            gcol_ref[dst] = ga[:, width // 2:].reshape(BIG, cols, width // 2)
            return c
        lax.fori_loop(0, rows // BIG, finish, 0)


def mlp(mid, grad, halo, edge, gain, w_up, conv_kernel, w_down, w_out):
    rows, cols, width = mid.shape
    hidden = w_up.shape[1]
    held = rows + 8
    trips = (rows + 4 + GROUP) // GROUP + 2
    slots = (GROUP * trips + GUARD + 1) * STRIDE
    whole = pl.BlockSpec(memory_space=pltpu.VMEM)
    half = jax.ShapeDtypeStruct((rows, cols, width // 2), BF16)
    return pl.pallas_call(
        functools.partial(mlp_kernel, rows, cols),
        out_shape=(jax.ShapeDtypeStruct((rows, cols, width), BF16), half, half),
        grid=(hidden // FC,),
        in_specs=[whole, whole, whole, whole, whole,
                  pl.BlockSpec((width, FC), lambda i: (0, i)),
                  pl.BlockSpec((9, FC), lambda i: (0, i)),
                  pl.BlockSpec((FC, width), lambda i: (i, 0)),
                  whole],
        out_specs=(whole, whole, whole),
        scratch_shapes=[
            pltpu.VMEM((3, held * STRIDE, width), BF16),
            pltpu.VMEM((3, slots, FC), BF16),
            pltpu.VMEM((slots, FC), BF16),
            pltpu.VMEM((3, slots, width), F32),
            pltpu.VMEM((width, FC), BF16),
            pltpu.VMEM((FC, width), BF16),
            pltpu.VMEM(((rows + 10) * STRIDE, width), BF16),
        ],
        compiler_params=pltpu.CompilerParams(vmem_limit_bytes=60 * 1024 * 1024),
        cost_estimate=pl.CostEstimate(flops=20_000_000_000, transcendentals=4_000_000, bytes_accessed=12_000_000),
        name="mlp_backward",
    )(mid, grad, halo, edge, gain.reshape(1, -1), w_up, conv_kernel, w_down, w_out)


def attn_kernel(nl, nk, half, split, mask_ref, *refs):
    (x_ref, g_ref, gain_ref, wq_ref, wk_ref, wv_ref, out_ref, w_s, wt_s,
     q_s, k_s, v_s, g_s, kt_s, qmt_s, qm_s, gmt_s, gm_s, e_s, dp_s, st_s, dq_s, dk_s, dv_s) = refs if not split else refs[:1] + refs[:1] + refs[1:]
    heads = HEADS // 2
    hw = 128
    hd = hw // heads
    length = nk * BLK
    factor = hd ** -0.5
    gain = gain_ref[...]
    wide = heads * BLK

    qmt_s[...] = jnp.zeros_like(qmt_s)
    gmt_s[...] = jnp.zeros_like(gmt_s)
    dk_s[...] = jnp.zeros_like(dk_s)
    dv_s[...] = jnp.zeros_like(dv_s)

    for j, ref in enumerate((wq_ref, wk_ref, wv_ref)):
        part = ref[:, half * hw:(half + 1) * hw]
        w_s[:, j * hw:(j + 1) * hw] = part
        wt_s[j * hw:(j + 1) * hw, :] = part.astype(F32).T.astype(BF16)

    def prepare(line, carry):
        xv = (x_ref[:, line, :, :2 * hw] if split else x_ref[:, line]).reshape(length, 2 * hw).astype(F32)
        mean = jnp.mean(xv, axis=-1, keepdims=True)
        center = xv - mean
        inv = lax.rsqrt(jnp.mean(center * center, axis=-1, keepdims=True) + EPSILON)
        normed = (center * inv * gain).astype(BF16)
        qkv = jnp.dot(normed, w_s[...], preferred_element_type=F32)
        kf = qkv[:, hw:2 * hw]
        q_s[line] = (qkv[:, :hw] * (factor * LOG2E)).astype(BF16)
        k_s[line] = kf.astype(BF16)
        v_s[line] = qkv[:, 2 * hw:].astype(BF16)
        kt_s[line] = kf.T.astype(BF16)
        g_s[line] = (g_ref[:, line, :, 2 * hw:] if split else g_ref[:, line]).reshape(length, hw)
        return carry

    lax.fori_loop(0, nl, prepare, 0)
    lane = lax.broadcasted_iota(jnp.int32, (BLK, hw), 1)

    def query_block(qb, carry):
        qs = pl.ds(pl.multiple_of(qb * BLK, BLK), BLK)
        for line in range(nl):
            for src, dt, dm in ((q_s, qmt_s, qm_s), (g_s, gmt_s, gm_s)):
                blk = src[line, qs, :]
                blk_f = blk.astype(F32)
                blk_t = blk_f.T.astype(BF16)
                for h in range(heads):
                    dt[line, h * hd:(h + 1) * hd, h * BLK:(h + 1) * BLK] = blk_t[h * hd:(h + 1) * hd]
                    inside = (lane >= h * hd) & (lane < (h + 1) * hd)
                    dm[line, h * BLK:(h + 1) * BLK, :] = jnp.where(inside, blk_f, 0.0).astype(BF16)

        def phase_a(kb, c):
            allowed = mask_ref[qb, kb] > 0
            ks = pl.ds(pl.multiple_of(kb * BLK, BLK), BLK)

            @pl.when(jnp.logical_not(allowed))
            def _():
                for line in range(nl):
                    st_s[kb, line] = jnp.concatenate(
                        [jnp.full((1, wide), -jnp.inf, F32), jnp.zeros((7, wide), F32)], axis=0)

            @pl.when(allowed)
            def _():
                for line in range(nl):
                    s = jnp.dot(k_s[line, ks, :], qmt_s[line], preferred_element_type=F32)
                    dp = jnp.dot(v_s[line, ks, :], gmt_s[line], preferred_element_type=F32)
                    top = jnp.max(s, axis=0, keepdims=True)
                    e = jnp.exp2(s - top)
                    e_s[kb, line] = e.astype(BF16)
                    dp_s[kb, line] = dp
                    st_s[kb, line, 0:1] = top
                    st_s[kb, line, 1:2] = jnp.sum(e, axis=0, keepdims=True)
                    st_s[kb, line, 2:3] = jnp.sum(e * dp, axis=0, keepdims=True)
            return c

        lax.fori_loop(0, nk, phase_a, 0)

        for line in range(nl):
            top = st_s[0, line, 0:1]
            for kb in range(1, nk):
                top = jnp.maximum(top, st_s[kb, line, 0:1])
            total = jnp.zeros((1, wide), F32)
            moment = jnp.zeros((1, wide), F32)
            weights = []
            for kb in range(nk):
                wk = jnp.exp2(st_s[kb, line, 0:1] - top)
                weights.append(wk)
                total = total + wk * st_s[kb, line, 1:2]
                moment = moment + wk * st_s[kb, line, 2:3]
            inv = 1.0 / total
            delta = moment * inv
            for kb in range(nk):
                st_s[kb, line, 3:4] = weights[kb] * inv
                st_s[kb, line, 4:5] = delta
            dq_s[line] = jnp.zeros((hd, wide), F32)

        def phase_b(kb, c):
            ks = pl.ds(pl.multiple_of(kb * BLK, BLK), BLK)

            @pl.when(mask_ref[qb, kb] > 0)
            def _():
                for line in range(nl):
                    p = e_s[kb, line].astype(F32) * st_s[kb, line, 3:4]
                    ds = (p * (dp_s[kb, line] - st_s[kb, line, 4:5])).astype(BF16)
                    dv_s[line, ks, :] += jnp.dot(p.astype(BF16), gm_s[line], preferred_element_type=F32)
                    dk_s[line, ks, :] += jnp.dot(ds, qm_s[line], preferred_element_type=F32)
                    for h in range(heads):
                        dq_s[line, :, h * BLK:(h + 1) * BLK] += jnp.dot(
                            kt_s[line, h * hd:(h + 1) * hd, ks], ds[:, h * BLK:(h + 1) * BLK],
                            preferred_element_type=F32)
            return c

        lax.fori_loop(0, nk, phase_b, 0)
        for line in range(nl):
            full = jnp.concatenate([dq_s[line, :, h * BLK:(h + 1) * BLK] for h in range(heads)], axis=0)
            q_s[line, qs, :] = (full.T * factor).astype(BF16)
        return carry

    lax.fori_loop(0, nk, query_block, 0)

    def finish(line, carry):
        grads = jnp.concatenate(
            [q_s[line], (dk_s[line] * LN2).astype(BF16), dv_s[line].astype(BF16)], axis=1)
        res = jnp.dot(grads, wt_s[...], preferred_element_type=F32).astype(BF16)
        out_ref[:, line] = res.reshape(out_ref.shape[0], out_ref.shape[2], out_ref.shape[3])
        return carry

    lax.fori_loop(0, nl, finish, 0)


def attention(arrays, gain, w_query, w_key, w_value, mask, half):
    srcs, nl, span = arrays[0].shape[:3]
    width = w_query.shape[0]
    length = srcs * span
    nk = length // BLK
    hw = width // 2
    heads = HEADS // 2
    wide = heads * BLK
    vm = pl.BlockSpec(memory_space=pltpu.VMEM)
    pairs = nk * nk * nl
    return pl.pallas_call(
        functools.partial(attn_kernel, nl, nk, half, len(arrays) == 1),
        out_shape=jax.ShapeDtypeStruct((srcs, nl, span, width), BF16),
        in_specs=[pl.BlockSpec(memory_space=pltpu.SMEM)] + [vm] * (len(arrays) + 4),
        out_specs=vm,
        scratch_shapes=[
            pltpu.VMEM((width, 3 * hw), BF16),
            pltpu.VMEM((3 * hw, width), BF16),
            pltpu.VMEM((nl, length, hw), BF16),
            pltpu.VMEM((nl, length, hw), BF16),
            pltpu.VMEM((nl, length, hw), BF16),
            pltpu.VMEM((nl, length, hw), BF16),
            pltpu.VMEM((nl, hw, length), BF16),
            pltpu.VMEM((nl, hw, wide), BF16),
            pltpu.VMEM((nl, wide, hw), BF16),
            pltpu.VMEM((nl, hw, wide), BF16),
            pltpu.VMEM((nl, wide, hw), BF16),
            pltpu.VMEM((nk, nl, BLK, wide), BF16),
            pltpu.VMEM((nk, nl, BLK, wide), F32),
            pltpu.VMEM((nk, nl, 8, wide), F32),
            pltpu.VMEM((nl, hw // heads, wide), F32),
            pltpu.VMEM((nl, length, hw), F32),
            pltpu.VMEM((nl, length, hw), F32),
        ],
        compiler_params=pltpu.CompilerParams(vmem_limit_bytes=40 * 1024 * 1024),
        cost_estimate=pl.CostEstimate(flops=pairs * 200_000_000, transcendentals=pairs * 65536, bytes_accessed=4_000_000),
        name="axial_attention",
    )(mask, *arrays, gain.reshape(1, -1), w_query, w_key, w_value)


def final_kernel(tok_ref, mid_ref, row_ref, col_ref, gain_ref, out_ref):
    count, cols, width = tok_ref.shape

    def flat(ref):
        return ref[...].reshape(count * cols, width).astype(F32)

    hat, inv = normalize(flat(tok_ref))
    e = (flat(row_ref) + flat(col_ref)) * gain_ref[...]
    res = flat(mid_ref) + inv * (
        e - jnp.mean(e, axis=-1, keepdims=True) - hat * jnp.mean(e * hat, axis=-1, keepdims=True))
    out_ref[...] = res.astype(BF16).reshape(count, cols, width)


def final(tokens, grad_mid, row_back, col_back, gain):
    rows, cols, width = tokens.shape
    blk = pl.BlockSpec((8, cols, width), lambda i: (i, 0, 0))
    return pl.pallas_call(
        final_kernel,
        out_shape=jax.ShapeDtypeStruct(tokens.shape, BF16),
        grid=(rows // 8,),
        in_specs=[blk, blk, blk, blk, pl.BlockSpec((1, width), lambda i: (0, 0))],
        out_specs=blk,
        cost_estimate=pl.CostEstimate(flops=20_000_000, transcendentals=4_000, bytes_accessed=8_000_000),
        name="norm_backward",
    )(tokens, grad_mid, row_back, col_back, gain.reshape(1, -1))


def to_lines(blocks, axis):
    return lax.all_to_all(blocks, axis, split_axis=0, concat_axis=0, tiled=True)


def cut_cols(tile, count):
    rows, cols, width = tile.shape
    return jnp.transpose(tile.reshape(rows, count, cols // count, width), (1, 2, 0, 3))


def neighbours(ahead, behind, axis):
    count = lax.axis_size(axis)
    up = [(i, i + 1) for i in range(count - 1)]
    return lax.ppermute(ahead, axis, up), lax.ppermute(behind, axis, [(j, i) for i, j in up])


def per_device(tokens_in, saved_mid, grad_out, attn_gain, mlp_gain, w_query, w_key, w_value, w_out,
               w_up, conv_kernel, w_down, row_mask, col_mask):
    rows, cols, width = tokens_in.shape
    half = width // 2
    count_gx = lax.axis_size("gx")
    count_gy = lax.axis_size("gy")

    def both(rs, cs):
        return jnp.concatenate([saved_mid[rs, cs], grad_out[rs, cs]], axis=-1)

    every = slice(None)
    above, below = neighbours(both(slice(rows - 2, rows), every), both(slice(0, 2), every), "gy")
    row_tokens = to_lines(tokens_in.reshape(count_gx, rows // count_gx, cols, width), "gx")
    sides = [jnp.concatenate([above[:, cs], both(every, cs), below[:, cs]], axis=0)
             for cs in (slice(cols - 2, cols), slice(0, 2))]
    left, right = neighbours(sides[0], sides[1], "gx")
    edge = jnp.concatenate([
        jnp.pad(right, ((2, 4), (0, 0), (0, 0))),
        jnp.zeros((rows + 10, STRIDE - cols - 4, 2 * width), BF16),
        jnp.pad(left, ((1, 5), (0, 0), (0, 0)))], axis=1)
    halo = jnp.concatenate([above, below], axis=0)
    grad_mid, grad_row, grad_col = mlp(
        saved_mid, grad_out, halo, edge, mlp_gain, w_up, conv_kernel, w_down, w_out)
    hold = lax.optimization_barrier
    grad_row, row_tokens = hold((grad_row, row_tokens))
    grad_row = to_lines(grad_row.reshape(count_gx, rows // count_gx, cols, half), "gx")
    col_send = cut_cols(jnp.concatenate([tokens_in, grad_col], axis=-1), count_gy)
    grad_row, col_send = hold((grad_row, col_send))
    col_lines = to_lines(col_send, "gy")
    weights = (w_query, w_key, w_value)
    row_out = attention((row_tokens, grad_row), attn_gain, *weights, row_mask, 0)
    row_out, col_lines = hold((row_out, col_lines))
    row_back = to_lines(row_out, "gx").reshape(rows, cols, width)
    col_out = attention((col_lines,), attn_gain, *weights, col_mask, 1)
    row_back, col_out = hold((row_back, col_out))
    col_back = jnp.transpose(to_lines(col_out, "gy"), (2, 0, 1, 3)).reshape(rows, cols, width)
    return final(tokens_in, grad_mid, row_back, col_back, attn_gain)


def solution(mesh):
    tile = P("gy", "gx", None)
    return jax.shard_map(per_device, mesh=mesh, in_specs=(tile,) * 3 + (P(),) * 11, out_specs=tile, check_vma=False)
```

```python
import functools

import jax
import jax.numpy as jnp
from jax import lax
from jax.experimental import pallas as pl
from jax.experimental.pallas import tpu as pltpu
from jax.sharding import PartitionSpec as P

HEADS = 8
BLK = 128
EPSILON = 1e-05
GELU_C = 0.7978845608028654
LOG2E = 1.4426950408889634
LN2 = 0.6931471805599453
F32 = jnp.float32
BF16 = jnp.bfloat16
STRIDE = 64
GROUP = 4
CHUNK = GROUP * STRIDE
BIG = 8
GUARD = 2 * GROUP + 4
FC = 256


def dot_nt(a, b):
    return lax.dot_general(a, b, (((1,), (1,)), ((), ())), preferred_element_type=F32)


def gelu_slope(v):
    k = lambda x: jnp.asarray(x, v.dtype)
    u = v * v
    t = jnp.tanh(v * (k(GELU_C) + k(GELU_C * 0.044715) * u))
    poly = v * (k(0.5 * GELU_C) + k(1.5 * 0.044715 * GELU_C) * u)
    return (k(0.5) + k(0.5) * t) + (k(1.0) - t * t) * poly


def normalize(x):
    center = x - jnp.mean(x, axis=-1, keepdims=True)
    inv = lax.rsqrt(jnp.mean(center * center, axis=-1, keepdims=True) + EPSILON)
    return center * inv, inv


def mlp_kernel(rows, cols, mid_ref, gout_ref, tok_ref, rowh_ref, edge_ref, gain_ref, wup_ref, conv_ref, wdown_ref, wout_ref,
               gm_ref, grow_ref, gcol_ref, x_s, h_s, gp_s, y_s, wdt_s, wut_s, grad_s):
    step = pl.program_id(0)
    width = mid_ref.shape[-1]
    gain = gain_ref[...]
    held = rows + 8
    trips = (rows + 4 + GROUP) // GROUP + 2
    tall = BIG * STRIDE

    def rows_at(row):
        return pl.multiple_of(row * STRIDE, STRIDE)

    @pl.when(step == 0)
    def _():
        edges = STRIDE - cols

        def place(ref, lead, row, values, count):
            for j in range(values.shape[0] // count):
                start = (row + j) * STRIDE + (0 if count == cols else cols)
                ref[lead + (pl.ds(pl.multiple_of(start, 16), count), slice(None))] = values[j * count:(j + 1) * count]

        def scaled(values):
            return normalize(values.astype(F32))[0] * gain

        none = jnp.zeros((cols, width), F32)
        for row in (0, 1, rows + 6, rows + 7, rows + 8, rows + 9):
            place(y_s, (0,), row, none, cols)
            place(grad_s, (), row, none.astype(BF16), cols)
        halo = rowh_ref[...].reshape(4 * cols, 2 * width)
        for part, row in ((0, 2), (1, rows + 4)):
            values = halo[part * 2 * cols:(part + 1) * 2 * cols]
            place(y_s, (0,), row, scaled(values[:, :width]), cols)
            place(grad_s, (), row, values[:, width:], cols)

        def edge_block(i, c):
            n = (rows + 10) // 2
            values = edge_ref[pl.ds(i * n, n)].reshape(n * edges, 2 * width)
            place(y_s, (0,), i * n, scaled(values[:, :width]), edges)
            place(grad_s, (), i * n, values[:, width:], edges)
            return c
        lax.fori_loop(0, 2, edge_block, 0)

        def norm_block(i, c):
            src = pl.ds(i * BIG, BIG)
            place(y_s, (0,), i * BIG + 4, scaled(mid_ref[src].reshape(BIG * cols, width)), cols)
            place(grad_s, (), i * BIG + 4, gout_ref[src].reshape(BIG * cols, width), cols)
            return c
        lax.fori_loop(0, rows // BIG, norm_block, 0)

        def shift_block(i, c):
            at = rows_at(i * BIG + 1)
            xv = y_s[0, pl.ds(at, tall + 8), :]
            lv = y_s[0, pl.ds(at - 8, tall + 8), :]
            dst = pl.ds(rows_at(i * BIG), tall)
            x_s[0, dst, :] = lv[7:7 + tall].astype(BF16)
            x_s[1, dst, :] = xv[:tall].astype(BF16)
            x_s[2, dst, :] = xv[1:1 + tall].astype(BF16)
            return c
        lax.fori_loop(0, held // BIG, shift_block, 0)

    wdt_s[...] = wdown_ref[...].astype(F32).T.astype(BF16)
    wut_s[...] = wup_ref[...].astype(F32).T.astype(BF16)
    taps = [conv_ref[t:t + 1, :].astype(BF16) for t in range(9)]
    first = step == 0

    def body(i, c):
        z0 = GROUP * (i - 2) - 2 + GUARD
        for b in range(3):
            parts = []
            for sub in range(GROUP):
                z = None
                for a in range(3):
                    term = gp_s[pl.ds(rows_at(z0 + 1 - a + sub), STRIDE), :] * taps[3 * a + b]
                    z = term if z is None else z + term
                parts.append(z)
            old = y_s[b, pl.ds(rows_at(z0), CHUNK), :]
            y_s[b, pl.ds(rows_at(z0), CHUNK), :] = jnp.where(first, 0.0, old) + jnp.dot(
                jnp.concatenate(parts, axis=0), wut_s[...], preferred_element_type=F32)
        g0 = GROUP * (i - 1) - 1
        ga = jnp.dot(grad_s[pl.ds(rows_at(jnp.clip(g0 + 1, 0, held + 2 - GROUP)), CHUNK), :], wdt_s[...],
                     preferred_element_type=F32)
        for sub in range(GROUP):
            pre = None
            for a in range(3):
                for b in range(3):
                    term = h_s[b, pl.ds(rows_at(g0 + GUARD + a - 1 + sub), STRIDE), :] * taps[3 * a + b]
                    pre = term if pre is None else pre + term
            gp_s[pl.ds(rows_at(g0 + GUARD + sub), STRIDE), :] = (
                ga[sub * STRIDE:(sub + 1) * STRIDE] * gelu_slope(pre).astype(F32)).astype(BF16)
        src = pl.ds(rows_at(jnp.minimum(GROUP * i, held - GROUP)), CHUNK)
        for b in range(3):
            h_s[b, pl.ds(rows_at(GROUP * i + GUARD), CHUNK), :] = jnp.dot(
                x_s[b, src, :], wup_ref[...], preferred_element_type=F32).astype(BF16)
        return c

    lax.fori_loop(0, trips, body, 0)

    @pl.when(step == pl.num_programs(0) - 1)
    def _():
        def finish(i, c):
            base = rows_at(i * BIG + 3 + GUARD)
            right = y_s[0, pl.ds(base, tall + 8), :][1:1 + tall]
            left = y_s[2, pl.ds(base - 8, tall + 8), :][7:7 + tall]
            total = y_s[1, pl.ds(base, tall), :] + right + left

            def crop(v):
                return v.reshape(BIG, STRIDE, width)[:, :cols].reshape(BIG * cols, width)

            e = crop(total) * gain
            src = pl.ds(i * BIG, BIG)
            hat, inv = normalize(mid_ref[src].reshape(BIG * cols, width).astype(F32))
            res = gout_ref[src].reshape(BIG * cols, width).astype(F32) + inv * (
                e - jnp.mean(e, axis=-1, keepdims=True) - hat * jnp.mean(e * hat, axis=-1, keepdims=True))
            res = res.astype(BF16)
            dst = pl.ds(i * BIG, BIG)
            gm_ref[dst] = res.reshape(BIG, cols, width)
            ga = dot_nt(res, wout_ref[...]).astype(BF16)
            grow_ref[dst] = ga[:, :width // 2].reshape(BIG, cols, width // 2)
            gcol_ref[dst, :, width:] = ga[:, width // 2:].reshape(BIG, cols, width // 2)
            gcol_ref[dst, :, :width] = tok_ref[dst]
            return c
        lax.fori_loop(0, rows // BIG, finish, 0)


def mlp(mid, grad, tokens, halo, edge, gain, w_up, conv_kernel, w_down, w_out):
    rows, cols, width = mid.shape
    hidden = w_up.shape[1]
    held = rows + 8
    trips = (rows + 4 + GROUP) // GROUP + 2
    slots = (GROUP * trips + GUARD + 1) * STRIDE
    whole = pl.BlockSpec(memory_space=pltpu.VMEM)
    return pl.pallas_call(
        functools.partial(mlp_kernel, rows, cols),
        out_shape=tuple(jax.ShapeDtypeStruct((rows, cols, n), BF16) for n in (width, width // 2, width + width // 2)),
        grid=(hidden // FC,),
        in_specs=[whole, whole, whole, whole, whole, whole,
                  pl.BlockSpec((width, FC), lambda i: (0, i)),
                  pl.BlockSpec((9, FC), lambda i: (0, i)),
                  pl.BlockSpec((FC, width), lambda i: (i, 0)),
                  whole],
        out_specs=(whole, whole, whole),
        scratch_shapes=[
            pltpu.VMEM((3, held * STRIDE, width), BF16),
            pltpu.VMEM((3, slots, FC), BF16),
            pltpu.VMEM((slots, FC), BF16),
            pltpu.VMEM((3, slots, width), F32),
            pltpu.VMEM((width, FC), BF16),
            pltpu.VMEM((FC, width), BF16),
            pltpu.VMEM(((rows + 10) * STRIDE, width), BF16),
        ],
        compiler_params=pltpu.CompilerParams(vmem_limit_bytes=60 * 1024 * 1024),
        cost_estimate=pl.CostEstimate(flops=20_000_000_000, transcendentals=4_000_000, bytes_accessed=12_000_000),
        name="mlp_backward",
    )(mid, grad, tokens, halo, edge, gain.reshape(1, -1), w_up, conv_kernel, w_down, w_out)


def attn_kernel(nl, nk, half, pieces, mask_ref, at_ref, *refs):
    x_ref, g_ref = refs[:2]
    piece_refs = refs[:pieces]
    (gain_ref, wq_ref, wk_ref, wv_ref, out_ref, w_s, wt_s, q_s, k_s, v_s, g_s, kt_s, qmt_s, qm_s, gmt_s, gm_s,
     e_s, dp_s, st_s, dq_s, dk_s, dv_s) = refs[max(pieces, 2):]
    heads = HEADS // 2
    hw = 128
    hd = hw // heads
    length = nk * BLK
    factor = hd ** -0.5
    gain = gain_ref[...]
    wide = heads * BLK

    qmt_s[...] = jnp.zeros_like(qmt_s)
    gmt_s[...] = jnp.zeros_like(gmt_s)
    dk_s[...] = jnp.zeros_like(dk_s)
    dv_s[...] = jnp.zeros_like(dv_s)

    for j, ref in enumerate((wq_ref, wk_ref, wv_ref)):
        part = ref[:, half * hw:(half + 1) * hw]
        w_s[:, j * hw:(j + 1) * hw] = part
        wt_s[j * hw:(j + 1) * hw, :] = part.astype(F32).T.astype(BF16)

    def project(xv):
        normed = (normalize(xv.astype(F32))[0] * gain).astype(BF16)
        return jnp.dot(normed, w_s[...], preferred_element_type=F32)

    def keep(line, where, qkv, grads):
        q_s[line, where, :] = (qkv[:, :hw] * (factor * LOG2E)).astype(BF16)
        k_s[line, where, :] = qkv[:, hw:2 * hw].astype(BF16)
        v_s[line, where, :] = qkv[:, 2 * hw:].astype(BF16)
        g_s[line, where, :] = grads

    if pieces:
        span = out_ref.shape[2]
        for piece, ref in enumerate(piece_refs):
            where = pl.ds(pl.multiple_of(at_ref[piece] * span, span), span)
            qkv = project(ref[:, :, :2 * hw].reshape(nl * span, 2 * hw))
            for line in range(nl):
                keep(line, where, qkv[line * span:(line + 1) * span], ref[line, :, 2 * hw:])
    else:
        def prepare(line, carry):
            keep(line, slice(None), project(x_ref[:, line].reshape(length, 2 * hw)),
                 g_ref[:, line].reshape(length, hw))
            return carry
        lax.fori_loop(0, nl, prepare, 0)

    def turn(line, carry):
        kt_s[line] = k_s[line].astype(F32).T.astype(BF16)
        return carry
    lax.fori_loop(0, nl, turn, 0)
    lane = lax.broadcasted_iota(jnp.int32, (BLK, hw), 1)

    def query_block(qb, carry):
        qs = pl.ds(pl.multiple_of(qb * BLK, BLK), BLK)
        for line in range(nl):
            for src, dt, dm in ((q_s, qmt_s, qm_s), (g_s, gmt_s, gm_s)):
                blk = src[line, qs, :]
                blk_f = blk.astype(F32)
                blk_t = blk_f.T.astype(BF16)
                for h in range(heads):
                    dt[line, h * hd:(h + 1) * hd, h * BLK:(h + 1) * BLK] = blk_t[h * hd:(h + 1) * hd]
                    inside = (lane >= h * hd) & (lane < (h + 1) * hd)
                    dm[line, h * BLK:(h + 1) * BLK, :] = jnp.where(inside, blk_f, 0.0).astype(BF16)

        def phase_a(kb, c):
            allowed = mask_ref[qb, kb] > 0
            ks = pl.ds(pl.multiple_of(kb * BLK, BLK), BLK)

            @pl.when(jnp.logical_not(allowed))
            def _():
                for line in range(nl):
                    st_s[kb, line] = jnp.concatenate(
                        [jnp.full((1, wide), -jnp.inf, F32), jnp.zeros((7, wide), F32)], axis=0)

            @pl.when(allowed)
            def _():
                for line in range(nl):
                    s = jnp.dot(k_s[line, ks, :], qmt_s[line], preferred_element_type=F32)
                    dp = jnp.dot(v_s[line, ks, :], gmt_s[line], preferred_element_type=F32)
                    top = jnp.max(s, axis=0, keepdims=True)
                    e = jnp.exp2(s - top)
                    e_s[kb, line] = e.astype(BF16)
                    dp_s[kb, line] = dp
                    st_s[kb, line, 0:1] = top
                    st_s[kb, line, 1:2] = jnp.sum(e, axis=0, keepdims=True)
                    st_s[kb, line, 2:3] = jnp.sum(e * dp, axis=0, keepdims=True)
            return c

        lax.fori_loop(0, nk, phase_a, 0)

        for line in range(nl):
            top = st_s[0, line, 0:1]
            for kb in range(1, nk):
                top = jnp.maximum(top, st_s[kb, line, 0:1])
            total = jnp.zeros((1, wide), F32)
            moment = jnp.zeros((1, wide), F32)
            weights = []
            for kb in range(nk):
                wk = jnp.exp2(st_s[kb, line, 0:1] - top)
                weights.append(wk)
                total = total + wk * st_s[kb, line, 1:2]
                moment = moment + wk * st_s[kb, line, 2:3]
            inv = 1.0 / total
            delta = moment * inv
            for kb in range(nk):
                st_s[kb, line, 3:4] = weights[kb] * inv
                st_s[kb, line, 4:5] = delta
            dq_s[line] = jnp.zeros((hd, wide), F32)

        def phase_b(kb, c):
            ks = pl.ds(pl.multiple_of(kb * BLK, BLK), BLK)

            @pl.when(mask_ref[qb, kb] > 0)
            def _():
                for line in range(nl):
                    p = e_s[kb, line].astype(F32) * st_s[kb, line, 3:4]
                    ds = (p * (dp_s[kb, line] - st_s[kb, line, 4:5])).astype(BF16)
                    dv_s[line, ks, :] += jnp.dot(p.astype(BF16), gm_s[line], preferred_element_type=F32)
                    dk_s[line, ks, :] += jnp.dot(ds, qm_s[line], preferred_element_type=F32)
                    for h in range(heads):
                        dq_s[line, :, h * BLK:(h + 1) * BLK] += jnp.dot(
                            kt_s[line, h * hd:(h + 1) * hd, ks], ds[:, h * BLK:(h + 1) * BLK],
                            preferred_element_type=F32)
            return c

        lax.fori_loop(0, nk, phase_b, 0)
        for line in range(nl):
            full = jnp.concatenate([dq_s[line, :, h * BLK:(h + 1) * BLK] for h in range(heads)], axis=0)
            q_s[line, qs, :] = (full.T * factor).astype(BF16)
        return carry

    lax.fori_loop(0, nk, query_block, 0)

    def finish(line, carry):
        grads = jnp.concatenate(
            [q_s[line], (dk_s[line] * LN2).astype(BF16), dv_s[line].astype(BF16)], axis=1)
        res = jnp.dot(grads, wt_s[...], preferred_element_type=F32).astype(BF16)
        out_ref[:, line] = res.reshape(out_ref.shape[0], out_ref.shape[2], out_ref.shape[3])
        return carry

    lax.fori_loop(0, nl, finish, 0)


def attention(arrays, at, shape, gain, w_query, w_key, w_value, mask, half):
    srcs, nl, span = shape
    pieces = srcs if len(arrays) == srcs else 0
    width = w_query.shape[0]
    length = srcs * span
    nk = length // BLK
    hw = width // 2
    heads = HEADS // 2
    wide = heads * BLK
    vm = pl.BlockSpec(memory_space=pltpu.VMEM)
    pairs = nk * nk * nl
    return pl.pallas_call(
        functools.partial(attn_kernel, nl, nk, half, pieces),
        out_shape=jax.ShapeDtypeStruct((srcs, nl, span, width), BF16),
        in_specs=[pl.BlockSpec(memory_space=pltpu.SMEM)] * 2 + [vm] * (len(arrays) + 4),
        out_specs=vm,
        scratch_shapes=[
            pltpu.VMEM((width, 3 * hw), BF16),
            pltpu.VMEM((3 * hw, width), BF16),
            pltpu.VMEM((nl, length, hw), BF16),
            pltpu.VMEM((nl, length, hw), BF16),
            pltpu.VMEM((nl, length, hw), BF16),
            pltpu.VMEM((nl, length, hw), BF16),
            pltpu.VMEM((nl, hw, length), BF16),
            pltpu.VMEM((nl, hw, wide), BF16),
            pltpu.VMEM((nl, wide, hw), BF16),
            pltpu.VMEM((nl, hw, wide), BF16),
            pltpu.VMEM((nl, wide, hw), BF16),
            pltpu.VMEM((nk, nl, BLK, wide), BF16),
            pltpu.VMEM((nk, nl, BLK, wide), F32),
            pltpu.VMEM((nk, nl, 8, wide), F32),
            pltpu.VMEM((nl, hw // heads, wide), F32),
            pltpu.VMEM((nl, length, hw), F32),
            pltpu.VMEM((nl, length, hw), F32),
        ],
        compiler_params=pltpu.CompilerParams(vmem_limit_bytes=40 * 1024 * 1024),
        cost_estimate=pl.CostEstimate(flops=pairs * 200_000_000, transcendentals=pairs * 65536, bytes_accessed=4_000_000),
        name="axial_attention",
    )(mask, at, *arrays, gain.reshape(1, -1), w_query, w_key, w_value)


def final_kernel(tok_ref, mid_ref, row_ref, col_ref, gain_ref, out_ref):
    count, cols, width = tok_ref.shape

    def flat(ref):
        return ref[...].reshape(count * cols, width).astype(F32)

    hat, inv = normalize(flat(tok_ref))
    e = (flat(row_ref) + flat(col_ref)) * gain_ref[...]
    res = flat(mid_ref) + inv * (
        e - jnp.mean(e, axis=-1, keepdims=True) - hat * jnp.mean(e * hat, axis=-1, keepdims=True))
    out_ref[...] = res.astype(BF16).reshape(count, cols, width)


def final(tokens, grad_mid, row_back, col_back, gain):
    rows, cols, width = tokens.shape
    blk = pl.BlockSpec((8, cols, width), lambda i: (i, 0, 0))
    return pl.pallas_call(
        final_kernel,
        out_shape=jax.ShapeDtypeStruct(tokens.shape, BF16),
        grid=(rows // 8,),
        in_specs=[blk, blk, blk, blk, pl.BlockSpec((1, width), lambda i: (0, 0))],
        out_specs=blk,
        cost_estimate=pl.CostEstimate(flops=20_000_000, transcendentals=4_000, bytes_accessed=8_000_000),
        name="norm_backward",
    )(tokens, grad_mid, row_back, col_back, gain.reshape(1, -1))


def to_lines(blocks, axis):
    return lax.all_to_all(blocks, axis, split_axis=0, concat_axis=0, tiled=True)


def cut_cols(tile, count):
    rows, cols, width = tile.shape
    return jnp.transpose(tile.reshape(rows, count, cols // count, width), (1, 2, 0, 3))


def neighbours(ahead, behind, axis):
    count = lax.axis_size(axis)
    up = [(i, i + 1) for i in range(count - 1)]
    return lax.ppermute(ahead, axis, up), lax.ppermute(behind, axis, [(j, i) for i, j in up])


def per_device(tokens_in, saved_mid, grad_out, attn_gain, mlp_gain, w_query, w_key, w_value, w_out,
               w_up, conv_kernel, w_down, row_mask, col_mask):
    rows, cols, width = tokens_in.shape
    half = width // 2
    count_gx = lax.axis_size("gx")
    count_gy = lax.axis_size("gy")

    def both(rs, cs):
        return jnp.concatenate([saved_mid[rs, cs], grad_out[rs, cs]], axis=-1)

    every = slice(None)
    above, below = neighbours(both(slice(rows - 2, rows), every), both(slice(0, 2), every), "gy")
    row_tokens = to_lines(tokens_in.reshape(count_gx, rows // count_gx, cols, width), "gx")
    sides = [jnp.concatenate([above[:, cs], both(every, cs), below[:, cs]], axis=0)
             for cs in (slice(cols - 2, cols), slice(0, 2))]
    left, right = neighbours(sides[0], sides[1], "gx")
    edge = jnp.concatenate([
        jnp.pad(right, ((2, 4), (0, 0), (0, 0))),
        jnp.zeros((rows + 10, STRIDE - cols - 4, 2 * width), BF16),
        jnp.pad(left, ((1, 5), (0, 0), (0, 0)))], axis=1)
    halo = jnp.concatenate([above, below], axis=0)
    grad_mid, grad_row, grad_col = mlp(
        saved_mid, grad_out, tokens_in, halo, edge, mlp_gain, w_up, conv_kernel, w_down, w_out)
    hold = lax.optimization_barrier
    grad_row, row_tokens = hold((grad_row, row_tokens))
    grad_row = to_lines(grad_row.reshape(count_gx, rows // count_gx, cols, half), "gx")
    here = lax.axis_index("gy")
    col_send = cut_cols(grad_col, count_gy)
    col_parts = []
    for ahead in range(count_gy):
        part = lax.dynamic_index_in_dim(col_send, (here + ahead) % count_gy, 0, keepdims=False)
        if ahead:
            part = lax.ppermute(part, "gy", [(i, (i + ahead) % count_gy) for i in range(count_gy)])
        col_parts.append(part)
    col_at = (here - jnp.arange(count_gy, dtype=jnp.int32)) % count_gy
    weights = (w_query, w_key, w_value)
    row_out = attention((row_tokens, grad_row), col_at, (count_gx, rows // count_gx, cols), attn_gain, *weights,
                        row_mask, 0)
    row_out, *col_parts = hold((row_out, *col_parts))
    row_back = to_lines(row_out, "gx").reshape(rows, cols, width)
    col_out = attention(tuple(col_parts), col_at, (count_gy, cols // count_gy, rows), attn_gain, *weights,
                        col_mask, 1)
    row_back, col_out = hold((row_back, col_out))
    col_back = jnp.transpose(to_lines(col_out, "gy"), (2, 0, 1, 3)).reshape(rows, cols, width)
    return final(tokens_in, grad_mid, row_back, col_back, attn_gain)


def solution(mesh):
    tile = P("gy", "gx", None)
    return jax.shard_map(per_device, mesh=mesh, in_specs=(tile,) * 3 + (P(),) * 11, out_specs=tile, check_vma=False)
```

```python
import functools

import jax
import jax.numpy as jnp
from jax import lax
from jax.experimental import pallas as pl
from jax.experimental.pallas import tpu as pltpu
from jax.sharding import PartitionSpec as P

HEADS = 8
BLK = 128
EPSILON = 1e-05
GELU_C = 0.7978845608028654
LOG2E = 1.4426950408889634
LN2 = 0.6931471805599453
F32 = jnp.float32
BF16 = jnp.bfloat16
STRIDE = 64
GROUP = 8
CHUNK = GROUP * STRIDE
BIG = 8
GUARD = 2 * GROUP + 4
RING = 3 * GROUP
FC = 512


def dot_nt(a, b):
    return lax.dot_general(a, b, (((1,), (1,)), ((), ())), preferred_element_type=F32)


def gelu_slope(v):
    k = lambda x: jnp.asarray(x, v.dtype)
    u = v * v
    t = jnp.tanh(v * (k(GELU_C) + k(GELU_C * 0.044715) * u))
    poly = v * (k(0.5 * GELU_C) + k(1.5 * 0.044715 * GELU_C) * u)
    return (k(0.5) + k(0.5) * t) + (k(1.0) - t * t) * poly


def normalize(x):
    center = x - jnp.mean(x, axis=-1, keepdims=True)
    inv = lax.rsqrt(jnp.mean(center * center, axis=-1, keepdims=True) + EPSILON)
    return center * inv, inv


def mlp_kernel(rows, cols, mid_ref, gout_ref, tok_ref, rowh_ref, edge_ref, gain_ref, wup_ref, conv_ref, wdown_ref, wout_ref,
               gm_ref, grow_ref, gcol_ref, x_s, h_s, gp_s, y_s, wdt_s, wut_s, grad_s):
    width = mid_ref.shape[-1]
    gain = gain_ref[...]
    held = rows + 8
    trips = (rows + 4 + GROUP) // GROUP + 2
    tall = BIG * STRIDE

    def rows_at(row):
        return pl.multiple_of(row * STRIDE, STRIDE)

    edges = STRIDE - cols

    def place(ref, lead, row, values, count):
        for j in range(values.shape[0] // count):
            start = (row + j) * STRIDE + (0 if count == cols else cols)
            ref[lead + (pl.ds(pl.multiple_of(start, 16), count), slice(None))] = values[j * count:(j + 1) * count]

    def scaled(values):
        return normalize(values.astype(F32))[0] * gain

    none = jnp.zeros((cols, width), F32)
    for row in (0, 1, rows + 6, rows + 7, rows + 8, rows + 9):
        place(y_s, (0,), row, none, cols)
        place(grad_s, (), row, none.astype(BF16), cols)
    halo = rowh_ref[...].reshape(4 * cols, 2 * width)
    for part, row in ((0, 2), (1, rows + 4)):
        values = halo[part * 2 * cols:(part + 1) * 2 * cols]
        place(y_s, (0,), row, scaled(values[:, :width]), cols)
        place(grad_s, (), row, values[:, width:], cols)

    def edge_block(i, c):
        n = (rows + 10) // 2
        values = edge_ref[pl.ds(i * n, n)].reshape(n * edges, 2 * width)
        place(y_s, (0,), i * n, scaled(values[:, :width]), edges)
        place(grad_s, (), i * n, values[:, width:], edges)
        return c
    lax.fori_loop(0, 2, edge_block, 0)

    def norm_block(i, c):
        src = pl.ds(i * BIG, BIG)
        place(y_s, (0,), i * BIG + 4, scaled(mid_ref[src].reshape(BIG * cols, width)), cols)
        place(grad_s, (), i * BIG + 4, gout_ref[src].reshape(BIG * cols, width), cols)
        return c
    lax.fori_loop(0, rows // BIG, norm_block, 0)

    def shift_block(i, c):
        at = rows_at(i * BIG + 1)
        xv = y_s[0, pl.ds(at, tall + 8), :]
        lv = y_s[0, pl.ds(at - 8, tall + 8), :]
        dst = pl.ds(rows_at(i * BIG), tall)
        x_s[0, dst, :] = lv[7:7 + tall].astype(BF16)
        x_s[1, dst, :] = xv[:tall].astype(BF16)
        x_s[2, dst, :] = xv[1:1 + tall].astype(BF16)
        return c
    lax.fori_loop(0, held // BIG, shift_block, 0)

    wdt_s[...] = wdown_ref[...].astype(F32).T.astype(BF16)
    wut_s[...] = wup_ref[...].astype(F32).T.astype(BF16)
    taps = [conv_ref[t:t + 1, :].astype(BF16) for t in range(9)]
    hidden = wup_ref.shape[1]

    def slot(row):
        return pl.ds(rows_at(lax.rem(row + 2 * RING, RING)), STRIDE)

    def products(i):
        z0 = GROUP * (i - 2) - 2
        for b in range(3):
            parts = []
            for sub in range(GROUP):
                z = None
                for a in range(3):
                    term = gp_s[slot(z0 + 1 - a + sub), :] * taps[3 * a + b]
                    z = term if z is None else z + term
                parts.append(z)
            y_s[b, pl.ds(rows_at(z0 + GUARD), CHUNK), :] = jnp.dot(
                jnp.concatenate(parts, axis=0), wut_s[...], preferred_element_type=F32)

    def slopes(i):
        g0 = GROUP * (i - 1) - 1
        grads = grad_s[pl.ds(rows_at(jnp.clip(g0 + 1, 0, held + 2 - GROUP)), CHUNK), :]
        for at in range(0, hidden, FC):
            lanes = slice(at, at + FC)
            ga = jnp.dot(grads, wdt_s[:, lanes], preferred_element_type=F32)
            for sub in range(GROUP):
                pre = None
                for a in range(3):
                    for b in range(3):
                        term = h_s[b, slot(g0 + a - 1 + sub), lanes] * taps[3 * a + b][:, lanes]
                        pre = term if pre is None else pre + term
                gp_s[slot(g0 + sub), lanes] = (
                    ga[sub * STRIDE:(sub + 1) * STRIDE] * gelu_slope(pre).astype(F32)).astype(BF16)

    def project(i):
        src = pl.ds(rows_at(jnp.minimum(GROUP * i, held - GROUP)), CHUNK)
        dst = pl.ds(rows_at(lax.rem(GROUP * i, RING)), CHUNK)
        for b in range(3):
            for at in range(0, hidden, FC):
                lanes = slice(at, at + FC)
                h_s[b, dst, lanes] = jnp.dot(
                    x_s[b, src, :], wup_ref[:, lanes], preferred_element_type=F32).astype(BF16)

    def body(i, c):
        products(i)
        slopes(i)
        project(i)
        return c

    project(0)
    slopes(1)
    project(1)
    lax.fori_loop(2, trips - 2, body, 0)
    products(trips - 2)
    slopes(trips - 2)
    products(trips - 1)

    def finish(i, c):
        base = rows_at(i * BIG + 3 + GUARD)
        right = y_s[0, pl.ds(base, tall + 8), :][1:1 + tall]
        left = y_s[2, pl.ds(base - 8, tall + 8), :][7:7 + tall]
        total = y_s[1, pl.ds(base, tall), :] + right + left

        def crop(v):
            return v.reshape(BIG, STRIDE, width)[:, :cols].reshape(BIG * cols, width)

        e = crop(total) * gain
        src = pl.ds(i * BIG, BIG)
        hat, inv = normalize(mid_ref[src].reshape(BIG * cols, width).astype(F32))
        res = gout_ref[src].reshape(BIG * cols, width).astype(F32) + inv * (
            e - jnp.mean(e, axis=-1, keepdims=True) - hat * jnp.mean(e * hat, axis=-1, keepdims=True))
        res = res.astype(BF16)
        dst = pl.ds(i * BIG, BIG)
        gm_ref[dst] = res.reshape(BIG, cols, width)
        ga = dot_nt(res, wout_ref[...]).astype(BF16)
        grow_ref[dst] = ga[:, :width // 2].reshape(BIG, cols, width // 2)
        gcol_ref[dst, :, width:] = ga[:, width // 2:].reshape(BIG, cols, width // 2)
        gcol_ref[dst, :, :width] = tok_ref[dst]
        return c
    lax.fori_loop(0, rows // BIG, finish, 0)


def mlp(mid, grad, tokens, halo, edge, gain, w_up, conv_kernel, w_down, w_out):
    rows, cols, width = mid.shape
    hidden = w_up.shape[1]
    held = rows + 8
    trips = (rows + 4 + GROUP) // GROUP + 2
    slots = (GROUP * trips + GUARD + 1) * STRIDE
    whole = pl.BlockSpec(memory_space=pltpu.VMEM)
    return pl.pallas_call(
        functools.partial(mlp_kernel, rows, cols),
        out_shape=tuple(jax.ShapeDtypeStruct((rows, cols, n), BF16) for n in (width, width // 2, width + width // 2)),
        in_specs=[whole] * 10,
        out_specs=(whole, whole, whole),
        scratch_shapes=[
            pltpu.VMEM((3, held * STRIDE, width), BF16),
            pltpu.VMEM((3, RING * STRIDE, hidden), BF16),
            pltpu.VMEM((RING * STRIDE, hidden), BF16),
            pltpu.VMEM((3, slots, width), F32),
            pltpu.VMEM((width, hidden), BF16),
            pltpu.VMEM((hidden, width), BF16),
            pltpu.VMEM(((rows + 10) * STRIDE, width), BF16),
        ],
        compiler_params=pltpu.CompilerParams(vmem_limit_bytes=60 * 1024 * 1024),
        cost_estimate=pl.CostEstimate(flops=20_000_000_000, transcendentals=4_000_000, bytes_accessed=12_000_000),
        name="mlp_backward",
    )(mid, grad, tokens, halo, edge, gain.reshape(1, -1), w_up, conv_kernel, w_down, w_out)


def attn_kernel(nl, nk, half, pieces, mask_ref, at_ref, *refs):
    x_ref, g_ref = refs[:2]
    piece_refs = refs[:pieces]
    (gain_ref, wq_ref, wk_ref, wv_ref, out_ref, w_s, wt_s, q_s, k_s, v_s, g_s, kt_s, qmt_s, qm_s, gmt_s, gm_s,
     e_s, dp_s, st_s, dq_s, dk_s, dv_s) = refs[max(pieces, 2):]
    heads = HEADS // 2
    hw = 128
    hd = hw // heads
    length = nk * BLK
    factor = hd ** -0.5
    gain = gain_ref[...]
    wide = heads * BLK

    qmt_s[...] = jnp.zeros_like(qmt_s)
    gmt_s[...] = jnp.zeros_like(gmt_s)
    dk_s[...] = jnp.zeros_like(dk_s)
    dv_s[...] = jnp.zeros_like(dv_s)

    for j, ref in enumerate((wq_ref, wk_ref, wv_ref)):
        part = ref[:, half * hw:(half + 1) * hw]
        w_s[:, j * hw:(j + 1) * hw] = part
        wt_s[j * hw:(j + 1) * hw, :] = part.astype(F32).T.astype(BF16)

    def project(xv):
        normed = (normalize(xv.astype(F32))[0] * gain).astype(BF16)
        return jnp.dot(normed, w_s[...], preferred_element_type=F32)

    def keep(line, where, qkv, grads):
        q_s[line, where, :] = (qkv[:, :hw] * (factor * LOG2E)).astype(BF16)
        k_s[line, where, :] = qkv[:, hw:2 * hw].astype(BF16)
        v_s[line, where, :] = qkv[:, 2 * hw:].astype(BF16)
        g_s[line, where, :] = grads

    if pieces:
        span = out_ref.shape[2]
        for piece, ref in enumerate(piece_refs):
            where = pl.ds(pl.multiple_of(at_ref[piece] * span, span), span)
            qkv = project(ref[:, :, :2 * hw].reshape(nl * span, 2 * hw))
            for line in range(nl):
                keep(line, where, qkv[line * span:(line + 1) * span], ref[line, :, 2 * hw:])
    else:
        def prepare(line, carry):
            keep(line, slice(None), project(x_ref[:, line].reshape(length, 2 * hw)),
                 g_ref[:, line].reshape(length, hw))
            return carry
        lax.fori_loop(0, nl, prepare, 0)

    def turn(line, carry):
        kt_s[line] = k_s[line].astype(F32).T.astype(BF16)
        return carry
    lax.fori_loop(0, nl, turn, 0)
    lane = lax.broadcasted_iota(jnp.int32, (BLK, hw), 1)

    def query_block(qb, carry):
        qs = pl.ds(pl.multiple_of(qb * BLK, BLK), BLK)
        for line in range(nl):
            for src, dt, dm in ((q_s, qmt_s, qm_s), (g_s, gmt_s, gm_s)):
                blk = src[line, qs, :]
                blk_f = blk.astype(F32)
                blk_t = blk_f.T.astype(BF16)
                for h in range(heads):
                    dt[line, h * hd:(h + 1) * hd, h * BLK:(h + 1) * BLK] = blk_t[h * hd:(h + 1) * hd]
                    inside = (lane >= h * hd) & (lane < (h + 1) * hd)
                    dm[line, h * BLK:(h + 1) * BLK, :] = jnp.where(inside, blk_f, 0.0).astype(BF16)

        def phase_a(kb, c):
            allowed = mask_ref[qb, kb] > 0
            ks = pl.ds(pl.multiple_of(kb * BLK, BLK), BLK)

            @pl.when(jnp.logical_not(allowed))
            def _():
                for line in range(nl):
                    st_s[kb, line] = jnp.concatenate(
                        [jnp.full((1, wide), -jnp.inf, F32), jnp.zeros((7, wide), F32)], axis=0)

            @pl.when(allowed)
            def _():
                for line in range(nl):
                    s = jnp.dot(k_s[line, ks, :], qmt_s[line], preferred_element_type=F32)
                    dp = jnp.dot(v_s[line, ks, :], gmt_s[line], preferred_element_type=F32)
                    top = jnp.max(s, axis=0, keepdims=True)
                    e = jnp.exp2(s - top)
                    e_s[kb, line] = e.astype(BF16)
                    dp_s[kb, line] = dp
                    st_s[kb, line, 0:1] = top
                    st_s[kb, line, 1:2] = jnp.sum(e, axis=0, keepdims=True)
                    st_s[kb, line, 2:3] = jnp.sum(e * dp, axis=0, keepdims=True)
            return c

        lax.fori_loop(0, nk, phase_a, 0)

        for line in range(nl):
            top = st_s[0, line, 0:1]
            for kb in range(1, nk):
                top = jnp.maximum(top, st_s[kb, line, 0:1])
            total = jnp.zeros((1, wide), F32)
            moment = jnp.zeros((1, wide), F32)
            weights = []
            for kb in range(nk):
                wk = jnp.exp2(st_s[kb, line, 0:1] - top)
                weights.append(wk)
                total = total + wk * st_s[kb, line, 1:2]
                moment = moment + wk * st_s[kb, line, 2:3]
            inv = 1.0 / total
            delta = moment * inv
            for kb in range(nk):
                st_s[kb, line, 3:4] = weights[kb] * inv
                st_s[kb, line, 4:5] = delta
            dq_s[line] = jnp.zeros((hd, wide), F32)

        def phase_b(kb, c):
            ks = pl.ds(pl.multiple_of(kb * BLK, BLK), BLK)

            @pl.when(mask_ref[qb, kb] > 0)
            def _():
                for line in range(nl):
                    p = e_s[kb, line].astype(F32) * st_s[kb, line, 3:4]
                    ds = (p * (dp_s[kb, line] - st_s[kb, line, 4:5])).astype(BF16)
                    dv_s[line, ks, :] += jnp.dot(p.astype(BF16), gm_s[line], preferred_element_type=F32)
                    dk_s[line, ks, :] += jnp.dot(ds, qm_s[line], preferred_element_type=F32)
                    for h in range(heads):
                        dq_s[line, :, h * BLK:(h + 1) * BLK] += jnp.dot(
                            kt_s[line, h * hd:(h + 1) * hd, ks], ds[:, h * BLK:(h + 1) * BLK],
                            preferred_element_type=F32)
            return c

        lax.fori_loop(0, nk, phase_b, 0)
        for line in range(nl):
            full = jnp.concatenate([dq_s[line, :, h * BLK:(h + 1) * BLK] for h in range(heads)], axis=0)
            q_s[line, qs, :] = (full.T * factor).astype(BF16)
        return carry

    lax.fori_loop(0, nk, query_block, 0)

    def finish(line, carry):
        grads = jnp.concatenate(
            [q_s[line], (dk_s[line] * LN2).astype(BF16), dv_s[line].astype(BF16)], axis=1)
        res = jnp.dot(grads, wt_s[...], preferred_element_type=F32).astype(BF16)
        out_ref[:, line] = res.reshape(out_ref.shape[0], out_ref.shape[2], out_ref.shape[3])
        return carry

    lax.fori_loop(0, nl, finish, 0)


def attention(arrays, at, shape, gain, w_query, w_key, w_value, mask, half):
    srcs, nl, span = shape
    pieces = srcs if len(arrays) == srcs else 0
    width = w_query.shape[0]
    length = srcs * span
    nk = length // BLK
    hw = width // 2
    heads = HEADS // 2
    wide = heads * BLK
    vm = pl.BlockSpec(memory_space=pltpu.VMEM)
    pairs = nk * nk * nl
    return pl.pallas_call(
        functools.partial(attn_kernel, nl, nk, half, pieces),
        out_shape=jax.ShapeDtypeStruct((srcs, nl, span, width), BF16),
        in_specs=[pl.BlockSpec(memory_space=pltpu.SMEM)] * 2 + [vm] * (len(arrays) + 4),
        out_specs=vm,
        scratch_shapes=[
            pltpu.VMEM((width, 3 * hw), BF16),
            pltpu.VMEM((3 * hw, width), BF16),
            pltpu.VMEM((nl, length, hw), BF16),
            pltpu.VMEM((nl, length, hw), BF16),
            pltpu.VMEM((nl, length, hw), BF16),
            pltpu.VMEM((nl, length, hw), BF16),
            pltpu.VMEM((nl, hw, length), BF16),
            pltpu.VMEM((nl, hw, wide), BF16),
            pltpu.VMEM((nl, wide, hw), BF16),
            pltpu.VMEM((nl, hw, wide), BF16),
            pltpu.VMEM((nl, wide, hw), BF16),
            pltpu.VMEM((nk, nl, BLK, wide), BF16),
            pltpu.VMEM((nk, nl, BLK, wide), F32),
            pltpu.VMEM((nk, nl, 8, wide), F32),
            pltpu.VMEM((nl, hw // heads, wide), F32),
            pltpu.VMEM((nl, length, hw), F32),
            pltpu.VMEM((nl, length, hw), F32),
        ],
        compiler_params=pltpu.CompilerParams(vmem_limit_bytes=40 * 1024 * 1024),
        cost_estimate=pl.CostEstimate(flops=pairs * 200_000_000, transcendentals=pairs * 65536, bytes_accessed=4_000_000),
        name="axial_attention",
    )(mask, at, *arrays, gain.reshape(1, -1), w_query, w_key, w_value)


def final_kernel(tok_ref, mid_ref, row_ref, col_ref, gain_ref, out_ref):
    count, cols, width = tok_ref.shape

    def flat(ref):
        return ref[...].reshape(count * cols, width).astype(F32)

    hat, inv = normalize(flat(tok_ref))
    e = (flat(row_ref) + flat(col_ref)) * gain_ref[...]
    res = flat(mid_ref) + inv * (
        e - jnp.mean(e, axis=-1, keepdims=True) - hat * jnp.mean(e * hat, axis=-1, keepdims=True))
    out_ref[...] = res.astype(BF16).reshape(count, cols, width)


def final(tokens, grad_mid, row_back, col_back, gain):
    rows, cols, width = tokens.shape
    blk = pl.BlockSpec((16, cols, width), lambda i: (i, 0, 0))
    return pl.pallas_call(
        final_kernel,
        out_shape=jax.ShapeDtypeStruct(tokens.shape, BF16),
        grid=(rows // 16,),
        in_specs=[blk, blk, blk, blk, pl.BlockSpec((1, width), lambda i: (0, 0))],
        out_specs=blk,
        cost_estimate=pl.CostEstimate(flops=20_000_000, transcendentals=4_000, bytes_accessed=8_000_000),
        name="norm_backward",
    )(tokens, grad_mid, row_back, col_back, gain.reshape(1, -1))


def to_lines(blocks, axis):
    return lax.all_to_all(blocks, axis, split_axis=0, concat_axis=0, tiled=True)


def cut_cols(tile, count):
    rows, cols, width = tile.shape
    return jnp.transpose(tile.reshape(rows, count, cols // count, width), (1, 2, 0, 3))


def neighbours(ahead, behind, axis):
    count = lax.axis_size(axis)
    up = [(i, i + 1) for i in range(count - 1)]
    return lax.ppermute(ahead, axis, up), lax.ppermute(behind, axis, [(j, i) for i, j in up])


def per_device(tokens_in, saved_mid, grad_out, attn_gain, mlp_gain, w_query, w_key, w_value, w_out,
               w_up, conv_kernel, w_down, row_mask, col_mask):
    rows, cols, width = tokens_in.shape
    half = width // 2
    count_gx = lax.axis_size("gx")
    count_gy = lax.axis_size("gy")

    def both(rs, cs):
        return jnp.concatenate([saved_mid[rs, cs], grad_out[rs, cs]], axis=-1)

    every = slice(None)
    above, below = neighbours(both(slice(rows - 2, rows), every), both(slice(0, 2), every), "gy")
    row_tokens = to_lines(tokens_in.reshape(count_gx, rows // count_gx, cols, width), "gx")
    sides = [jnp.concatenate([above[:, cs], both(every, cs), below[:, cs]], axis=0)
             for cs in (slice(cols - 2, cols), slice(0, 2))]
    left, right = neighbours(sides[0], sides[1], "gx")
    edge = jnp.concatenate([
        jnp.pad(right, ((2, 4), (0, 0), (0, 0))),
        jnp.zeros((rows + 10, STRIDE - cols - 4, 2 * width), BF16),
        jnp.pad(left, ((1, 5), (0, 0), (0, 0)))], axis=1)
    halo = jnp.concatenate([above, below], axis=0)
    grad_mid, grad_row, grad_col = mlp(
        saved_mid, grad_out, tokens_in, halo, edge, mlp_gain, w_up, conv_kernel, w_down, w_out)
    hold = lax.optimization_barrier
    grad_row, row_tokens = hold((grad_row, row_tokens))
    grad_row = to_lines(grad_row.reshape(count_gx, rows // count_gx, cols, half), "gx")
    here = lax.axis_index("gy")
    col_send = cut_cols(grad_col, count_gy)
    col_parts = []
    for ahead in range(count_gy):
        part = lax.dynamic_index_in_dim(col_send, (here + ahead) % count_gy, 0, keepdims=False)
        if ahead:
            part = lax.ppermute(part, "gy", [(i, (i + ahead) % count_gy) for i in range(count_gy)])
        col_parts.append(part)
    col_at = (here - jnp.arange(count_gy, dtype=jnp.int32)) % count_gy
    weights = (w_query, w_key, w_value)
    row_out = attention((row_tokens, grad_row), col_at, (count_gx, rows // count_gx, cols), attn_gain, *weights,
                        row_mask, 0)
    row_out, *col_parts = hold((row_out, *col_parts))
    row_back = to_lines(row_out, "gx").reshape(rows, cols, width)
    col_out = attention(tuple(col_parts), col_at, (count_gy, cols // count_gy, rows), attn_gain, *weights,
                        col_mask, 1)
    row_back, col_out = hold((row_back, col_out))
    col_back = jnp.transpose(to_lines(col_out, "gy"), (2, 0, 1, 3)).reshape(rows, cols, width)
    return final(tokens_in, grad_mid, row_back, col_back, attn_gain)


def solution(mesh):
    tile = P("gy", "gx", None)
    return jax.shard_map(per_device, mesh=mesh, in_specs=(tile,) * 3 + (P(),) * 11, out_specs=tile, check_vma=False)
```

```python
import functools

import jax
import jax.numpy as jnp
from jax import lax
from jax.experimental import pallas as pl
from jax.experimental.pallas import tpu as pltpu
from jax.sharding import PartitionSpec as P

HEADS = 8
BLK = 128
EPSILON = 1e-05
GELU_C = 0.7978845608028654
LOG2E = 1.4426950408889634
LN2 = 0.6931471805599453
F32 = jnp.float32
BF16 = jnp.bfloat16
STRIDE = 64
GROUP = 8
CHUNK = GROUP * STRIDE
BIG = 8
GUARD = 2
RING = 3 * GROUP
FC = 512


def dot_nt(a, b):
    return lax.dot_general(a, b, (((1,), (1,)), ((), ())), preferred_element_type=F32)


def gelu_slope(v):
    k = lambda x: jnp.asarray(x, v.dtype)
    u = v * v
    t = jnp.tanh(v * (k(GELU_C) + k(GELU_C * 0.044715) * u))
    poly = v * (k(0.5 * GELU_C) + k(1.5 * 0.044715 * GELU_C) * u)
    return (k(0.5) + k(0.5) * t) + (k(1.0) - t * t) * poly


def normalize(x):
    center = x - jnp.mean(x, axis=-1, keepdims=True)
    inv = lax.rsqrt(jnp.mean(center * center, axis=-1, keepdims=True) + EPSILON)
    return center * inv, inv


def mlp_kernel(rows, cols, mid_ref, gout_ref, tok_ref, above_ref, below_ref, edge_ref, gain_ref, wup_ref, conv_ref, wdown_ref, wout_ref,
               wq_ref, wk_ref, wv_ref,
               gm_ref, grow_ref, gcol_ref, wide_ref, x_s, h_s, gp_s, y_s, wdt_s, wut_s, grad_s):
    width = mid_ref.shape[-1]
    gain = gain_ref[...]
    held = rows + 8
    trips = (rows + 4 + GROUP) // GROUP + 2
    tall = BIG * STRIDE

    def rows_at(row):
        return pl.multiple_of(row * STRIDE, STRIDE)

    edges = STRIDE - cols

    def place(ref, lead, row, values, count):
        for j in range(values.shape[0] // count):
            start = (row + j) * STRIDE + (0 if count == cols else cols)
            ref[lead + (pl.ds(pl.multiple_of(start, 16), count), slice(None))] = values[j * count:(j + 1) * count]

    def scaled(values):
        return normalize(values.astype(F32))[0] * gain

    none = jnp.zeros((cols, width), F32)
    for row in (0, 1, rows + 6, rows + 7, rows + 8, rows + 9):
        place(y_s, (0,), row, none, cols)
        place(grad_s, (), row, none.astype(BF16), cols)
    for ref, row in ((above_ref, 2), (below_ref, rows + 4)):
        values = ref[...].reshape(2 * cols, 2 * width)
        place(y_s, (0,), row, scaled(values[:, :width]), cols)
        place(grad_s, (), row, values[:, width:], cols)

    def edge_block(i, c):
        n = (rows + 10) // 2
        values = edge_ref[pl.ds(i * n, n)].reshape(n * edges, 2 * width)
        place(y_s, (0,), i * n, scaled(values[:, :width]), edges)
        place(grad_s, (), i * n, values[:, width:], edges)
        return c
    lax.fori_loop(0, 2, edge_block, 0)

    def norm_block(i, c):
        src = pl.ds(i * BIG, BIG)
        place(y_s, (0,), i * BIG + 4, scaled(mid_ref[src].reshape(BIG * cols, width)), cols)
        place(grad_s, (), i * BIG + 4, gout_ref[src].reshape(BIG * cols, width), cols)
        return c
    lax.fori_loop(0, rows // BIG, norm_block, 0)

    def shift_block(i, c):
        at = rows_at(i * BIG + 1)
        xv = y_s[0, pl.ds(at, tall + 8), :]
        lv = y_s[0, pl.ds(at - 8, tall + 8), :]
        dst = pl.ds(rows_at(i * BIG), tall)
        x_s[0, dst, :] = lv[7:7 + tall].astype(BF16)
        x_s[1, dst, :] = xv[:tall].astype(BF16)
        x_s[2, dst, :] = xv[1:1 + tall].astype(BF16)
        return c
    lax.fori_loop(0, held // BIG, shift_block, 0)

    n = width // 2
    for half in range(2):
        for j, ref in enumerate((wq_ref, wk_ref, wv_ref)):
            wide_ref[half, :, j * n:(j + 1) * n] = ref[:, half * n:(half + 1) * n]
    wdt_s[...] = wdown_ref[...].astype(F32).T.astype(BF16)
    wut_s[...] = wup_ref[...].astype(F32).T.astype(BF16)
    taps = [conv_ref[t:t + 1, :].astype(BF16) for t in range(9)]
    hidden = wup_ref.shape[1]

    def slot(row):
        return pl.ds(rows_at(lax.rem(row + 2 * RING, RING)), STRIDE)

    def products(i):
        z0 = GROUP * (i - 2) - 2
        for b in range(3):
            parts = []
            for sub in range(GROUP):
                z = None
                for a in range(3):
                    term = gp_s[slot(z0 + 1 - a + sub), :] * taps[3 * a + b]
                    z = term if z is None else z + term
                parts.append(z)
            y_s[b, pl.ds(rows_at(z0 + GUARD), CHUNK), :] = jnp.dot(
                jnp.concatenate(parts, axis=0), wut_s[...], preferred_element_type=F32)

    def slopes(i):
        g0 = GROUP * (i - 1) - 1
        grads = grad_s[pl.ds(rows_at(jnp.clip(g0 + 1, 0, held + 2 - GROUP)), CHUNK), :]
        for at in range(0, hidden, FC):
            lanes = slice(at, at + FC)
            ga = jnp.dot(grads, wdt_s[:, lanes], preferred_element_type=F32)
            for sub in range(GROUP):
                pre = None
                for a in range(3):
                    for b in range(3):
                        term = h_s[b, slot(g0 + a - 1 + sub), lanes] * taps[3 * a + b][:, lanes]
                        pre = term if pre is None else pre + term
                gp_s[slot(g0 + sub), lanes] = (
                    ga[sub * STRIDE:(sub + 1) * STRIDE] * gelu_slope(pre).astype(F32)).astype(BF16)

    def project(i):
        src = pl.ds(rows_at(jnp.minimum(GROUP * i, held - GROUP)), CHUNK)
        dst = pl.ds(rows_at(lax.rem(GROUP * i, RING)), CHUNK)
        for b in range(3):
            for at in range(0, hidden, FC):
                lanes = slice(at, at + FC)
                h_s[b, dst, lanes] = jnp.dot(
                    x_s[b, src, :], wup_ref[:, lanes], preferred_element_type=F32).astype(BF16)

    def body(i, c):
        products(i)
        slopes(i)
        project(i)
        return c

    project(0)
    slopes(1)
    project(1)
    lax.fori_loop(2, trips - 2, body, 0)
    products(trips - 2)
    slopes(trips - 2)
    products(trips - 1)

    def finish(i, c):
        base = rows_at(i * BIG + 3 + GUARD)
        right = y_s[0, pl.ds(base, tall + 8), :][1:1 + tall]
        left = y_s[2, pl.ds(base - 8, tall + 8), :][7:7 + tall]
        total = y_s[1, pl.ds(base, tall), :] + right + left

        def crop(v):
            return v.reshape(BIG, STRIDE, width)[:, :cols].reshape(BIG * cols, width)

        e = crop(total) * gain
        src = pl.ds(i * BIG, BIG)
        hat, inv = normalize(mid_ref[src].reshape(BIG * cols, width).astype(F32))
        res = gout_ref[src].reshape(BIG * cols, width).astype(F32) + inv * (
            e - jnp.mean(e, axis=-1, keepdims=True) - hat * jnp.mean(e * hat, axis=-1, keepdims=True))
        res = res.astype(BF16)
        dst = pl.ds(i * BIG, BIG)
        gm_ref[dst] = res.reshape(BIG, cols, width)
        ga = dot_nt(res, wout_ref[...]).astype(BF16)
        grow_ref[dst] = ga[:, :width // 2].reshape(BIG, cols, width // 2)
        gcol_ref[dst, :, width:] = ga[:, width // 2:].reshape(BIG, cols, width // 2)
        gcol_ref[dst, :, :width] = tok_ref[dst]
        return c
    lax.fori_loop(0, rows // BIG, finish, 0)


def mlp(mid, grad, tokens, above, below, edge, gain, w_up, conv_kernel, w_down, w_out, w_query, w_key, w_value):
    rows, cols, width = mid.shape
    hidden = w_up.shape[1]
    held = rows + 8
    trips = (rows + 4 + GROUP) // GROUP + 2
    slots = max(GROUP * (trips - 2), rows + 12) * STRIDE
    whole = pl.BlockSpec(memory_space=pltpu.VMEM)
    return pl.pallas_call(
        functools.partial(mlp_kernel, rows, cols),
        out_shape=tuple(jax.ShapeDtypeStruct((rows, cols, n), BF16) for n in (width, width // 2, width + width // 2)) + (
            jax.ShapeDtypeStruct((2, width, 3 * width // 2), BF16),),
        in_specs=[whole] * 14,
        out_specs=(whole,) * 4,
        scratch_shapes=[
            pltpu.VMEM((3, held * STRIDE, width), BF16),
            pltpu.VMEM((3, RING * STRIDE, hidden), BF16),
            pltpu.VMEM((RING * STRIDE, hidden), BF16),
            pltpu.VMEM((3, slots, width), F32),
            pltpu.VMEM((width, hidden), BF16),
            pltpu.VMEM((hidden, width), BF16),
            pltpu.VMEM(((rows + 10) * STRIDE, width), BF16),
        ],
        compiler_params=pltpu.CompilerParams(vmem_limit_bytes=54 * 1024 * 1024),
        cost_estimate=pl.CostEstimate(flops=20_000_000_000, transcendentals=4_000_000, bytes_accessed=12_000_000),
        name="mlp_backward",
    )(mid, grad, tokens, above, below, edge, gain.reshape(1, -1), w_up, conv_kernel, w_down, w_out,
      w_query, w_key, w_value)


def attn_kernel(nl, nk, half, pieces, mask_ref, at_ref, *refs):
    x_ref, g_ref = refs[:2]
    piece_refs = refs[:pieces]
    (gain_ref, w_ref, out_ref, q_s, k_s, v_s, g_s, kt_s, qmt_s, qm_s, gmt_s, gm_s,
     e_s, dp_s, st_s, dq_s, dk_s, dv_s) = refs[max(pieces, 2):]
    heads = HEADS // 2
    hw = 128
    hd = hw // heads
    length = nk * BLK
    factor = hd ** -0.5
    gain = gain_ref[...]
    wide = heads * BLK

    qmt_s[...] = jnp.zeros_like(qmt_s)
    gmt_s[...] = jnp.zeros_like(gmt_s)
    dk_s[...] = jnp.zeros_like(dk_s)
    dv_s[...] = jnp.zeros_like(dv_s)

    def project(xv):
        normed = (normalize(xv.astype(F32))[0] * gain).astype(BF16)
        return jnp.dot(normed, w_ref[half], preferred_element_type=F32)

    def keep(line, where, qkv, grads):
        q_s[line, where, :] = (qkv[:, :hw] * (factor * LOG2E)).astype(BF16)
        k_s[line, where, :] = qkv[:, hw:2 * hw].astype(BF16)
        v_s[line, where, :] = qkv[:, 2 * hw:].astype(BF16)
        g_s[line, where, :] = grads

    if pieces:
        span = out_ref.shape[2]
        for piece, ref in enumerate(piece_refs):
            where = pl.ds(pl.multiple_of(at_ref[piece] * span, span), span)
            qkv = project(ref[:, :, :2 * hw].reshape(nl * span, 2 * hw))
            for line in range(nl):
                keep(line, where, qkv[line * span:(line + 1) * span], ref[line, :, 2 * hw:])
    else:
        def prepare(line, carry):
            keep(line, slice(None), project(x_ref[:, line].reshape(length, 2 * hw)),
                 g_ref[:, line].reshape(length, hw))
            return carry
        lax.fori_loop(0, nl, prepare, 0)

    def turn(line, carry):
        kt_s[line] = k_s[line].astype(F32).T.astype(BF16)
        return carry
    lax.fori_loop(0, nl, turn, 0)
    lane = lax.broadcasted_iota(jnp.int32, (BLK, hw), 1)

    def query_block(qb, carry):
        qs = pl.ds(pl.multiple_of(qb * BLK, BLK), BLK)
        for line in range(nl):
            for src, dt, dm in ((q_s, qmt_s, qm_s), (g_s, gmt_s, gm_s)):
                blk = src[line, qs, :]
                blk_f = blk.astype(F32)
                blk_t = blk_f.T.astype(BF16)
                for h in range(heads):
                    dt[line, h * hd:(h + 1) * hd, h * BLK:(h + 1) * BLK] = blk_t[h * hd:(h + 1) * hd]
                    inside = (lane >= h * hd) & (lane < (h + 1) * hd)
                    dm[line, h * BLK:(h + 1) * BLK, :] = jnp.where(inside, blk_f, 0.0).astype(BF16)

        def phase_a(kb, c):
            allowed = mask_ref[qb, kb] > 0
            ks = pl.ds(pl.multiple_of(kb * BLK, BLK), BLK)

            @pl.when(jnp.logical_not(allowed))
            def _():
                for line in range(nl):
                    st_s[kb, line] = jnp.concatenate(
                        [jnp.full((1, wide), -jnp.inf, F32), jnp.zeros((7, wide), F32)], axis=0)

            @pl.when(allowed)
            def _():
                for line in range(nl):
                    s = jnp.dot(k_s[line, ks, :], qmt_s[line], preferred_element_type=F32)
                    dp = jnp.dot(v_s[line, ks, :], gmt_s[line], preferred_element_type=F32)
                    top = jnp.max(s, axis=0, keepdims=True)
                    e = jnp.exp2(s - top)
                    e_s[kb, line] = e.astype(BF16)
                    dp_s[kb, line] = dp
                    st_s[kb, line, 0:1] = top
                    st_s[kb, line, 1:2] = jnp.sum(e, axis=0, keepdims=True)
                    st_s[kb, line, 2:3] = jnp.sum(e * dp, axis=0, keepdims=True)
            return c

        lax.fori_loop(0, nk, phase_a, 0)

        for line in range(nl):
            top = st_s[0, line, 0:1]
            for kb in range(1, nk):
                top = jnp.maximum(top, st_s[kb, line, 0:1])
            total = jnp.zeros((1, wide), F32)
            moment = jnp.zeros((1, wide), F32)
            weights = []
            for kb in range(nk):
                wk = jnp.exp2(st_s[kb, line, 0:1] - top)
                weights.append(wk)
                total = total + wk * st_s[kb, line, 1:2]
                moment = moment + wk * st_s[kb, line, 2:3]
            inv = 1.0 / total
            delta = moment * inv
            for kb in range(nk):
                st_s[kb, line, 3:4] = weights[kb] * inv
                st_s[kb, line, 4:5] = delta
            dq_s[line] = jnp.zeros((hd, wide), F32)

        def phase_b(kb, c):
            ks = pl.ds(pl.multiple_of(kb * BLK, BLK), BLK)

            @pl.when(mask_ref[qb, kb] > 0)
            def _():
                for line in range(nl):
                    p = e_s[kb, line].astype(F32) * st_s[kb, line, 3:4]
                    ds = (p * (dp_s[kb, line] - st_s[kb, line, 4:5])).astype(BF16)
                    dv_s[line, ks, :] += jnp.dot(p.astype(BF16), gm_s[line], preferred_element_type=F32)
                    dk_s[line, ks, :] += jnp.dot(ds, qm_s[line], preferred_element_type=F32)
                    for h in range(heads):
                        dq_s[line, :, h * BLK:(h + 1) * BLK] += jnp.dot(
                            kt_s[line, h * hd:(h + 1) * hd, ks], ds[:, h * BLK:(h + 1) * BLK],
                            preferred_element_type=F32)
            return c

        lax.fori_loop(0, nk, phase_b, 0)
        for line in range(nl):
            full = jnp.concatenate([dq_s[line, :, h * BLK:(h + 1) * BLK] for h in range(heads)], axis=0)
            q_s[line, qs, :] = (full.T * factor).astype(BF16)
        return carry

    lax.fori_loop(0, nk, query_block, 0)

    def finish(line, carry):
        grads = jnp.concatenate(
            [q_s[line], (dk_s[line] * LN2).astype(BF16), dv_s[line].astype(BF16)], axis=1)
        res = dot_nt(grads, w_ref[half]).astype(BF16)
        out_ref[:, line] = res.reshape(out_ref.shape[0], out_ref.shape[2], out_ref.shape[3])
        return carry

    lax.fori_loop(0, nl, finish, 0)


def attention(arrays, at, shape, gain, w_wide, mask, half):
    srcs, nl, span = shape
    pieces = srcs if len(arrays) == srcs else 0
    width = w_wide.shape[1]
    length = srcs * span
    nk = length // BLK
    hw = width // 2
    heads = HEADS // 2
    wide = heads * BLK
    vm = pl.BlockSpec(memory_space=pltpu.VMEM)
    pairs = nk * nk * nl
    return pl.pallas_call(
        functools.partial(attn_kernel, nl, nk, half, pieces),
        out_shape=jax.ShapeDtypeStruct((srcs, nl, span, width), BF16),
        in_specs=[pl.BlockSpec(memory_space=pltpu.SMEM)] * 2 + [vm] * (len(arrays) + 2),
        out_specs=vm,
        scratch_shapes=[
            pltpu.VMEM((nl, length, hw), BF16),
            pltpu.VMEM((nl, length, hw), BF16),
            pltpu.VMEM((nl, length, hw), BF16),
            pltpu.VMEM((nl, length, hw), BF16),
            pltpu.VMEM((nl, hw, length), BF16),
            pltpu.VMEM((nl, hw, wide), BF16),
            pltpu.VMEM((nl, wide, hw), BF16),
            pltpu.VMEM((nl, hw, wide), BF16),
            pltpu.VMEM((nl, wide, hw), BF16),
            pltpu.VMEM((nk, nl, BLK, wide), BF16),
            pltpu.VMEM((nk, nl, BLK, wide), F32),
            pltpu.VMEM((nk, nl, 8, wide), F32),
            pltpu.VMEM((nl, hw // heads, wide), F32),
            pltpu.VMEM((nl, length, hw), F32),
            pltpu.VMEM((nl, length, hw), F32),
        ],
        compiler_params=pltpu.CompilerParams(vmem_limit_bytes=28 * 1024 * 1024),
        cost_estimate=pl.CostEstimate(flops=pairs * 200_000_000, transcendentals=pairs * 65536, bytes_accessed=4_000_000),
        name="axial_attention",
    )(mask, at, *arrays, gain.reshape(1, -1), w_wide)


def final_kernel(tok_ref, mid_ref, row_ref, col_ref, gain_ref, out_ref):
    count, cols, width = tok_ref.shape

    def flat(ref):
        return ref[...].reshape(count * cols, width).astype(F32)

    hat, inv = normalize(flat(tok_ref))
    turned = jnp.swapaxes(col_ref[...].reshape(cols, count, width).astype(F32), 0, 1).reshape(count * cols, width)
    e = (flat(row_ref) + turned) * gain_ref[...]
    res = flat(mid_ref) + inv * (
        e - jnp.mean(e, axis=-1, keepdims=True) - hat * jnp.mean(e * hat, axis=-1, keepdims=True))
    out_ref[...] = res.astype(BF16).reshape(count, cols, width)


def final(tokens, grad_mid, row_back, col_back, gain):
    rows, cols, width = tokens.shape
    blk = pl.BlockSpec((16, cols, width), lambda i: (i, 0, 0))
    return pl.pallas_call(
        final_kernel,
        out_shape=jax.ShapeDtypeStruct(tokens.shape, BF16),
        grid=(rows // 16,),
        in_specs=[blk, blk, blk, pl.BlockSpec((*col_back.shape[:2], 16, width), lambda i: (0, 0, i, 0)), pl.BlockSpec((1, width), lambda i: (0, 0))],
        out_specs=blk,
        cost_estimate=pl.CostEstimate(flops=20_000_000, transcendentals=4_000, bytes_accessed=8_000_000),
        name="norm_backward",
    )(tokens, grad_mid, row_back, col_back, gain.reshape(1, -1))


def to_lines(blocks, axis):
    return lax.all_to_all(blocks, axis, split_axis=0, concat_axis=0, tiled=True)


def cut_cols(tile, count):
    rows, cols, width = tile.shape
    return jnp.transpose(tile.reshape(rows, count, cols // count, width), (1, 2, 0, 3))


def neighbours(ahead, behind, axis):
    count = lax.axis_size(axis)
    up = [(i, i + 1) for i in range(count - 1)]
    return lax.ppermute(ahead, axis, up), lax.ppermute(behind, axis, [(j, i) for i, j in up])


def per_device(tokens_in, saved_mid, grad_out, attn_gain, mlp_gain, w_query, w_key, w_value, w_out,
               w_up, conv_kernel, w_down, row_mask, col_mask):
    rows, cols, width = tokens_in.shape
    half = width // 2
    count_gx = lax.axis_size("gx")
    count_gy = lax.axis_size("gy")

    def both(rs, cs):
        return jnp.concatenate([saved_mid[rs, cs], grad_out[rs, cs]], axis=-1)

    every = slice(None)
    above, below = neighbours(both(slice(rows - 2, rows), every), both(slice(0, 2), every), "gy")
    row_tokens = to_lines(tokens_in.reshape(count_gx, rows // count_gx, cols, width), "gx")
    sides = [jnp.concatenate([above[:, cs], both(every, cs), below[:, cs]], axis=0)
             for cs in (slice(cols - 2, cols), slice(0, 2))]
    left, right = neighbours(sides[0], sides[1], "gx")
    edge = jnp.concatenate([
        jnp.pad(right, ((2, 4), (0, 0), (0, 0))),
        jnp.zeros((rows + 10, STRIDE - cols - 4, 2 * width), BF16),
        jnp.pad(left, ((1, 5), (0, 0), (0, 0)))], axis=1)
    grad_mid, grad_row, grad_col, weights = mlp(
        saved_mid, grad_out, tokens_in, above, below, edge, mlp_gain, w_up, conv_kernel, w_down, w_out,
        w_query, w_key, w_value)
    hold = lax.optimization_barrier
    grad_row, row_tokens = hold((grad_row, row_tokens))
    grad_row = to_lines(grad_row.reshape(count_gx, rows // count_gx, cols, half), "gx")
    here = lax.axis_index("gy")
    col_send = cut_cols(grad_col, count_gy)
    col_parts = []
    for ahead in range(count_gy):
        part = lax.dynamic_index_in_dim(col_send, (here + ahead) % count_gy, 0, keepdims=False)
        if ahead:
            part = lax.ppermute(part, "gy", [(i, (i + ahead) % count_gy) for i in range(count_gy)])
        col_parts.append(part)
    col_at = (here - jnp.arange(count_gy, dtype=jnp.int32)) % count_gy
    row_out = attention((row_tokens, grad_row), col_at, (count_gx, rows // count_gx, cols), attn_gain, weights,
                        row_mask, 0)
    row_out, *col_parts = hold((row_out, *col_parts))
    row_back = to_lines(row_out, "gx").reshape(rows, cols, width)
    col_out = attention(tuple(col_parts), col_at, (count_gy, cols // count_gy, rows), attn_gain, weights,
                        col_mask, 1)
    row_back, col_out = hold((row_back, col_out))
    col_back = to_lines(col_out, "gy")
    return final(tokens_in, grad_mid, row_back, col_back, attn_gain)


def solution(mesh):
    tile = P("gy", "gx", None)
    return jax.shard_map(per_device, mesh=mesh, in_specs=(tile,) * 3 + (P(),) * 11, out_specs=tile, check_vma=False)
```

```python
import functools

import jax
import jax.numpy as jnp
from jax import lax
from jax.experimental import pallas as pl
from jax.experimental.pallas import tpu as pltpu
from jax.sharding import PartitionSpec as P

HEADS = 8
BLK = 128
EPSILON = 1e-05
GELU_C = 0.7978845608028654
LOG2E = 1.4426950408889634
LN2 = 0.6931471805599453
F32 = jnp.float32
BF16 = jnp.bfloat16
STRIDE = 64
GROUP = 8
CHUNK = GROUP * STRIDE
BIG = 8
GUARD = 2
RING = 3 * GROUP
FC = 256


def dot_nt(a, b):
    return lax.dot_general(a, b, (((1,), (1,)), ((), ())), preferred_element_type=F32)


def gelu_slope(v):
    k = lambda x: jnp.asarray(x, v.dtype)
    u = v * v
    t = jnp.tanh(v * (k(GELU_C) + k(GELU_C * 0.044715) * u))
    poly = v * (k(0.5 * GELU_C) + k(1.5 * 0.044715 * GELU_C) * u)
    return (k(0.5) + k(0.5) * t) + (k(1.0) - t * t) * poly


def normalize(x):
    center = x - jnp.mean(x, axis=-1, keepdims=True)
    inv = lax.rsqrt(jnp.mean(center * center, axis=-1, keepdims=True) + EPSILON)
    return center * inv, inv


def mlp_kernel(rows, cols, mid_ref, gout_ref, tok_ref, above_ref, below_ref, edge_ref, gain_ref, wup_ref, conv_ref, wdown_ref, wout_ref,
               wq_ref, wk_ref, wv_ref,
               gm_ref, grow_ref, gcol_ref, wide_ref, x_s, y_s, wdt_s, wut_s, grad_s, *rings):
    width = mid_ref.shape[-1]
    gain = gain_ref[...]
    held = rows + 8
    trips = (rows + 4 + GROUP) // GROUP + 2
    tall = BIG * STRIDE

    def rows_at(row):
        return pl.multiple_of(row * STRIDE, STRIDE)

    edges = STRIDE - cols

    def place(ref, lead, row, values, count):
        for j in range(values.shape[0] // count):
            start = (row + j) * STRIDE + (0 if count == cols else cols)
            ref[lead + (pl.ds(pl.multiple_of(start, 16), count), slice(None))] = values[j * count:(j + 1) * count]

    def scaled(values):
        return normalize(values.astype(F32))[0] * gain

    none = jnp.zeros((cols, width), F32)
    for row in (0, 1, rows + 6, rows + 7, rows + 8, rows + 9):
        place(y_s, (0,), row, none, cols)
        place(grad_s, (), row, none.astype(BF16), cols)
    for ref, row in ((above_ref, 2), (below_ref, rows + 4)):
        values = ref[...].reshape(2 * cols, 2 * width)
        place(y_s, (0,), row, scaled(values[:, :width]), cols)
        place(grad_s, (), row, values[:, width:], cols)

    def edge_block(i, c):
        n = (rows + 10) // 2
        values = edge_ref[pl.ds(i * n, n)].reshape(n * edges, 2 * width)
        place(y_s, (0,), i * n, scaled(values[:, :width]), edges)
        place(grad_s, (), i * n, values[:, width:], edges)
        return c
    lax.fori_loop(0, 2, edge_block, 0)

    def norm_block(i, c):
        src = pl.ds(i * BIG, BIG)
        place(y_s, (0,), i * BIG + 4, scaled(mid_ref[src].reshape(BIG * cols, width)), cols)
        place(grad_s, (), i * BIG + 4, gout_ref[src].reshape(BIG * cols, width), cols)
        return c
    lax.fori_loop(0, rows // BIG, norm_block, 0)

    def shift_block(i, c):
        at = rows_at(i * BIG + 1)
        xv = y_s[0, pl.ds(at, tall + 8), :]
        lv = y_s[0, pl.ds(at - 8, tall + 8), :]
        dst = pl.ds(rows_at(i * BIG), tall)
        x_s[0, dst, :] = lv[7:7 + tall].astype(BF16)
        x_s[1, dst, :] = xv[:tall].astype(BF16)
        x_s[2, dst, :] = xv[1:1 + tall].astype(BF16)
        return c
    lax.fori_loop(0, held // BIG, shift_block, 0)

    n = width // 2
    for half in range(2):
        for j, ref in enumerate((wq_ref, wk_ref, wv_ref)):
            wide_ref[half, :, j * n:(j + 1) * n] = ref[:, half * n:(half + 1) * n]
    wdt_s[...] = wdown_ref[...].astype(F32).T.astype(BF16)
    wut_s[...] = wup_ref[...].astype(F32).T.astype(BF16)
    taps = [conv_ref[t:t + 1, :].astype(BF16) for t in range(9)]
    hidden = wup_ref.shape[1]
    parts_of = hidden // FC
    h_parts, gp_parts = rings[:parts_of], rings[parts_of:]

    def slot(row):
        return pl.ds(rows_at(lax.rem(row + 2 * RING, RING)), STRIDE)

    def products(i):
        z0 = GROUP * (i - 2) - 2
        for b in range(3):
            stack = []
            for part in range(parts_of):
                lanes = slice(part * FC, (part + 1) * FC)
                pile = []
                for sub in range(GROUP):
                    z = None
                    for a in range(3):
                        term = gp_parts[part][slot(z0 + 1 - a + sub), :] * taps[3 * a + b][:, lanes]
                        z = term if z is None else z + term
                    pile.append(z)
                stack.append(jnp.concatenate(pile, axis=0))
            y_s[b, pl.ds(rows_at(z0 + GUARD), CHUNK), :] = jnp.dot(
                jnp.concatenate(stack, axis=1), wut_s[...], preferred_element_type=F32)

    def slopes(i, part):
        g0 = GROUP * (i - 1) - 1
        h_s, gp_s = h_parts[part], gp_parts[part]
        grads = grad_s[pl.ds(rows_at(jnp.clip(g0 + 1, 0, held + 2 - GROUP)), CHUNK), :]
        lanes = slice(part * FC, (part + 1) * FC)
        ga = jnp.dot(grads, wdt_s[:, lanes], preferred_element_type=F32)
        for sub in range(GROUP):
            pre = None
            for a in range(3):
                for b in range(3):
                    term = h_s[b, slot(g0 + a - 1 + sub), :] * taps[3 * a + b][:, lanes]
                    pre = term if pre is None else pre + term
            gp_s[slot(g0 + sub), :] = (
                ga[sub * STRIDE:(sub + 1) * STRIDE] * gelu_slope(pre).astype(F32)).astype(BF16)

    def project(i, part):
        src = pl.ds(rows_at(jnp.minimum(GROUP * i, held - GROUP)), CHUNK)
        dst = pl.ds(rows_at(lax.rem(GROUP * i, RING)), CHUNK)
        lanes = slice(part * FC, (part + 1) * FC)
        for b in range(3):
            h_parts[part][b, dst, :] = jnp.dot(
                x_s[b, src, :], wup_ref[:, lanes], preferred_element_type=F32).astype(BF16)

    def body(i, c):
        products(i)
        for part in range(parts_of):
            slopes(i, part)
            project(i, part)
        return c

    for part in range(parts_of):
        project(0, part)
    for part in range(parts_of):
        slopes(1, part)
        project(1, part)
    lax.fori_loop(2, trips - 2, body, 0)
    products(trips - 2)
    for part in range(parts_of):
        slopes(trips - 2, part)
    products(trips - 1)

    def finish(i, c):
        base = rows_at(i * BIG + 3 + GUARD)
        right = y_s[0, pl.ds(base, tall + 8), :][1:1 + tall]
        left = y_s[2, pl.ds(base - 8, tall + 8), :][7:7 + tall]
        total = y_s[1, pl.ds(base, tall), :] + right + left

        def crop(v):
            return v.reshape(BIG, STRIDE, width)[:, :cols].reshape(BIG * cols, width)

        e = crop(total) * gain
        src = pl.ds(i * BIG, BIG)
        hat, inv = normalize(mid_ref[src].reshape(BIG * cols, width).astype(F32))
        res = gout_ref[src].reshape(BIG * cols, width).astype(F32) + inv * (
            e - jnp.mean(e, axis=-1, keepdims=True) - hat * jnp.mean(e * hat, axis=-1, keepdims=True))
        res = res.astype(BF16)
        dst = pl.ds(i * BIG, BIG)
        gm_ref[dst] = res.reshape(BIG, cols, width)
        ga = dot_nt(res, wout_ref[...]).astype(BF16)
        grow_ref[dst] = ga[:, :width // 2].reshape(BIG, cols, width // 2)
        gcol_ref[dst, :, width:] = ga[:, width // 2:].reshape(BIG, cols, width // 2)
        gcol_ref[dst, :, :width] = tok_ref[dst]
        return c
    lax.fori_loop(0, rows // BIG, finish, 0)


def mlp(mid, grad, tokens, above, below, edge, gain, w_up, conv_kernel, w_down, w_out, w_query, w_key, w_value):
    rows, cols, width = mid.shape
    hidden = w_up.shape[1]
    held = rows + 8
    trips = (rows + 4 + GROUP) // GROUP + 2
    slots = max(GROUP * (trips - 2), rows + 12) * STRIDE
    whole = pl.BlockSpec(memory_space=pltpu.VMEM)
    return pl.pallas_call(
        functools.partial(mlp_kernel, rows, cols),
        out_shape=tuple(jax.ShapeDtypeStruct((rows, cols, n), BF16) for n in (width, width // 2, width + width // 2)) + (
            jax.ShapeDtypeStruct((2, width, 3 * width // 2), BF16),),
        in_specs=[whole] * 14,
        out_specs=(whole,) * 4,
        scratch_shapes=[
            pltpu.VMEM((3, held * STRIDE, width), BF16),
            pltpu.VMEM((3, slots, width), F32),
            pltpu.VMEM((width, hidden), BF16),
            pltpu.VMEM((hidden, width), BF16),
            pltpu.VMEM(((rows + 10) * STRIDE, width), BF16),
        ] + [pltpu.VMEM((3, RING * STRIDE, FC), BF16)] * (hidden // FC)
        + [pltpu.VMEM((RING * STRIDE, FC), BF16)] * (hidden // FC),
        compiler_params=pltpu.CompilerParams(vmem_limit_bytes=54 * 1024 * 1024),
        cost_estimate=pl.CostEstimate(flops=20_000_000_000, transcendentals=4_000_000, bytes_accessed=12_000_000),
        name="mlp_backward",
    )(mid, grad, tokens, above, below, edge, gain.reshape(1, -1), w_up, conv_kernel, w_down, w_out,
      w_query, w_key, w_value)


def attn_kernel(nl, nk, half, pieces, mask_ref, at_ref, *refs):
    x_ref, g_ref = refs[:2]
    piece_refs = refs[:pieces]
    (gain_ref, w_ref, out_ref, q_s, k_s, v_s, g_s, kt_s, qmt_s, qm_s, gmt_s, gm_s,
     e_s, dp_s, st_s, dq_s, dk_s, dv_s) = refs[max(pieces, 2):]
    heads = HEADS // 2
    hw = 128
    hd = hw // heads
    length = nk * BLK
    factor = hd ** -0.5
    gain = gain_ref[...]
    wide = heads * BLK

    qmt_s[...] = jnp.zeros_like(qmt_s)
    gmt_s[...] = jnp.zeros_like(gmt_s)
    dk_s[...] = jnp.zeros_like(dk_s)
    dv_s[...] = jnp.zeros_like(dv_s)

    def project(xv):
        normed = (normalize(xv.astype(F32))[0] * gain).astype(BF16)
        return jnp.dot(normed, w_ref[half], preferred_element_type=F32)

    def keep(line, where, qkv, grads):
        q_s[line, where, :] = (qkv[:, :hw] * (factor * LOG2E)).astype(BF16)
        k_s[line, where, :] = qkv[:, hw:2 * hw].astype(BF16)
        v_s[line, where, :] = qkv[:, 2 * hw:].astype(BF16)
        g_s[line, where, :] = grads

    if pieces:
        span = out_ref.shape[2]
        for piece, ref in enumerate(piece_refs):
            where = pl.ds(pl.multiple_of(at_ref[piece] * span, span), span)
            qkv = project(ref[:, :, :2 * hw].reshape(nl * span, 2 * hw))
            for line in range(nl):
                keep(line, where, qkv[line * span:(line + 1) * span], ref[line, :, 2 * hw:])
    else:
        def prepare(line, carry):
            keep(line, slice(None), project(x_ref[:, line].reshape(length, 2 * hw)),
                 g_ref[:, line].reshape(length, hw))
            return carry
        lax.fori_loop(0, nl, prepare, 0)

    def turn(line, carry):
        kt_s[line] = k_s[line].astype(F32).T.astype(BF16)
        return carry
    lax.fori_loop(0, nl, turn, 0)
    lane = lax.broadcasted_iota(jnp.int32, (BLK, hw), 1)

    def query_block(qb, carry):
        qs = pl.ds(pl.multiple_of(qb * BLK, BLK), BLK)
        for line in range(nl):
            for src, dt, dm in ((q_s, qmt_s, qm_s), (g_s, gmt_s, gm_s)):
                blk = src[line, qs, :]
                blk_f = blk.astype(F32)
                blk_t = blk_f.T.astype(BF16)
                for h in range(heads):
                    dt[line, h * hd:(h + 1) * hd, h * BLK:(h + 1) * BLK] = blk_t[h * hd:(h + 1) * hd]
                    inside = (lane >= h * hd) & (lane < (h + 1) * hd)
                    dm[line, h * BLK:(h + 1) * BLK, :] = jnp.where(inside, blk_f, 0.0).astype(BF16)

        def phase_a(kb, c):
            allowed = mask_ref[qb, kb] > 0
            ks = pl.ds(pl.multiple_of(kb * BLK, BLK), BLK)

            @pl.when(jnp.logical_not(allowed))
            def _():
                for line in range(nl):
                    st_s[kb, line] = jnp.concatenate(
                        [jnp.full((1, wide), -jnp.inf, F32), jnp.zeros((7, wide), F32)], axis=0)

            @pl.when(allowed)
            def _():
                for line in range(nl):
                    s = jnp.dot(k_s[line, ks, :], qmt_s[line], preferred_element_type=F32)
                    dp = jnp.dot(v_s[line, ks, :], gmt_s[line], preferred_element_type=F32)
                    top = jnp.max(s, axis=0, keepdims=True)
                    e = jnp.exp2(s - top)
                    e_s[kb, line] = e.astype(BF16)
                    dp_s[kb, line] = dp
                    st_s[kb, line, 0:1] = top
                    st_s[kb, line, 1:2] = jnp.sum(e, axis=0, keepdims=True)
                    st_s[kb, line, 2:3] = jnp.sum(e * dp, axis=0, keepdims=True)
            return c

        lax.fori_loop(0, nk, phase_a, 0)

        for line in range(nl):
            top = st_s[0, line, 0:1]
            for kb in range(1, nk):
                top = jnp.maximum(top, st_s[kb, line, 0:1])
            total = jnp.zeros((1, wide), F32)
            moment = jnp.zeros((1, wide), F32)
            weights = []
            for kb in range(nk):
                wk = jnp.exp2(st_s[kb, line, 0:1] - top)
                weights.append(wk)
                total = total + wk * st_s[kb, line, 1:2]
                moment = moment + wk * st_s[kb, line, 2:3]
            inv = 1.0 / total
            delta = moment * inv
            for kb in range(nk):
                st_s[kb, line, 3:4] = weights[kb] * inv
                st_s[kb, line, 4:5] = delta
            dq_s[line] = jnp.zeros((hd, wide), F32)

        def phase_b(kb, c):
            ks = pl.ds(pl.multiple_of(kb * BLK, BLK), BLK)

            @pl.when(mask_ref[qb, kb] > 0)
            def _():
                for line in range(nl):
                    p = e_s[kb, line].astype(F32) * st_s[kb, line, 3:4]
                    ds = (p * (dp_s[kb, line] - st_s[kb, line, 4:5])).astype(BF16)
                    dv_s[line, ks, :] += jnp.dot(p.astype(BF16), gm_s[line], preferred_element_type=F32)
                    dk_s[line, ks, :] += jnp.dot(ds, qm_s[line], preferred_element_type=F32)
                    for h in range(heads):
                        dq_s[line, :, h * BLK:(h + 1) * BLK] += jnp.dot(
                            kt_s[line, h * hd:(h + 1) * hd, ks], ds[:, h * BLK:(h + 1) * BLK],
                            preferred_element_type=F32)
            return c

        lax.fori_loop(0, nk, phase_b, 0)
        for line in range(nl):
            full = jnp.concatenate([dq_s[line, :, h * BLK:(h + 1) * BLK] for h in range(heads)], axis=0)
            q_s[line, qs, :] = (full.T * factor).astype(BF16)
        return carry

    lax.fori_loop(0, nk, query_block, 0)

    def finish(line, carry):
        grads = jnp.concatenate(
            [q_s[line], (dk_s[line] * LN2).astype(BF16), dv_s[line].astype(BF16)], axis=1)
        res = dot_nt(grads, w_ref[half]).astype(BF16)
        out_ref[:, line] = res.reshape(out_ref.shape[0], out_ref.shape[2], out_ref.shape[3])
        return carry

    lax.fori_loop(0, nl, finish, 0)


def attention(arrays, at, shape, gain, w_wide, mask, half):
    srcs, nl, span = shape
    pieces = srcs if len(arrays) == srcs else 0
    width = w_wide.shape[1]
    length = srcs * span
    nk = length // BLK
    hw = width // 2
    heads = HEADS // 2
    wide = heads * BLK
    vm = pl.BlockSpec(memory_space=pltpu.VMEM)
    pairs = nk * nk * nl
    return pl.pallas_call(
        functools.partial(attn_kernel, nl, nk, half, pieces),
        out_shape=jax.ShapeDtypeStruct((srcs, nl, span, width), BF16),
        in_specs=[pl.BlockSpec(memory_space=pltpu.SMEM)] * 2 + [vm] * (len(arrays) + 2),
        out_specs=vm,
        scratch_shapes=[
            pltpu.VMEM((nl, length, hw), BF16),
            pltpu.VMEM((nl, length, hw), BF16),
            pltpu.VMEM((nl, length, hw), BF16),
            pltpu.VMEM((nl, length, hw), BF16),
            pltpu.VMEM((nl, hw, length), BF16),
            pltpu.VMEM((nl, hw, wide), BF16),
            pltpu.VMEM((nl, wide, hw), BF16),
            pltpu.VMEM((nl, hw, wide), BF16),
            pltpu.VMEM((nl, wide, hw), BF16),
            pltpu.VMEM((nk, nl, BLK, wide), BF16),
            pltpu.VMEM((nk, nl, BLK, wide), F32),
            pltpu.VMEM((nk, nl, 8, wide), F32),
            pltpu.VMEM((nl, hw // heads, wide), F32),
            pltpu.VMEM((nl, length, hw), F32),
            pltpu.VMEM((nl, length, hw), F32),
        ],
        compiler_params=pltpu.CompilerParams(vmem_limit_bytes=28 * 1024 * 1024),
        cost_estimate=pl.CostEstimate(flops=pairs * 200_000_000, transcendentals=pairs * 65536, bytes_accessed=4_000_000),
        name="axial_attention",
    )(mask, at, *arrays, gain.reshape(1, -1), w_wide)


def final_kernel(tok_ref, mid_ref, row_ref, col_ref, gain_ref, out_ref):
    count, cols, width = tok_ref.shape

    def flat(ref):
        return ref[...].reshape(count * cols, width).astype(F32)

    hat, inv = normalize(flat(tok_ref))
    turned = jnp.swapaxes(col_ref[...].reshape(cols, count, width).astype(F32), 0, 1).reshape(count * cols, width)
    e = (flat(row_ref) + turned) * gain_ref[...]
    res = flat(mid_ref) + inv * (
        e - jnp.mean(e, axis=-1, keepdims=True) - hat * jnp.mean(e * hat, axis=-1, keepdims=True))
    out_ref[...] = res.astype(BF16).reshape(count, cols, width)


def final(tokens, grad_mid, row_back, col_back, gain):
    rows, cols, width = tokens.shape
    blk = pl.BlockSpec((16, cols, width), lambda i: (i, 0, 0))
    return pl.pallas_call(
        final_kernel,
        out_shape=jax.ShapeDtypeStruct(tokens.shape, BF16),
        grid=(rows // 16,),
        in_specs=[blk, blk, blk, pl.BlockSpec((*col_back.shape[:2], 16, width), lambda i: (0, 0, i, 0)), pl.BlockSpec((1, width), lambda i: (0, 0))],
        out_specs=blk,
        cost_estimate=pl.CostEstimate(flops=20_000_000, transcendentals=4_000, bytes_accessed=8_000_000),
        name="norm_backward",
    )(tokens, grad_mid, row_back, col_back, gain.reshape(1, -1))


def to_lines(blocks, axis):
    return lax.all_to_all(blocks, axis, split_axis=0, concat_axis=0, tiled=True)


def cut_cols(tile, count):
    rows, cols, width = tile.shape
    return jnp.transpose(tile.reshape(rows, count, cols // count, width), (1, 2, 0, 3))


def neighbours(ahead, behind, axis):
    count = lax.axis_size(axis)
    up = [(i, i + 1) for i in range(count - 1)]
    return lax.ppermute(ahead, axis, up), lax.ppermute(behind, axis, [(j, i) for i, j in up])


def per_device(tokens_in, saved_mid, grad_out, attn_gain, mlp_gain, w_query, w_key, w_value, w_out,
               w_up, conv_kernel, w_down, row_mask, col_mask):
    rows, cols, width = tokens_in.shape
    half = width // 2
    count_gx = lax.axis_size("gx")
    count_gy = lax.axis_size("gy")

    def both(rs, cs):
        return jnp.concatenate([saved_mid[rs, cs], grad_out[rs, cs]], axis=-1)

    every = slice(None)
    above, below = neighbours(both(slice(rows - 2, rows), every), both(slice(0, 2), every), "gy")
    row_tokens = to_lines(tokens_in.reshape(count_gx, rows // count_gx, cols, width), "gx")
    sides = [jnp.concatenate([above[:, cs], both(every, cs), below[:, cs]], axis=0)
             for cs in (slice(cols - 2, cols), slice(0, 2))]
    left, right = neighbours(sides[0], sides[1], "gx")
    edge = jnp.concatenate([
        jnp.pad(right, ((2, 4), (0, 0), (0, 0))),
        jnp.zeros((rows + 10, STRIDE - cols - 4, 2 * width), BF16),
        jnp.pad(left, ((1, 5), (0, 0), (0, 0)))], axis=1)
    grad_mid, grad_row, grad_col, weights = mlp(
        saved_mid, grad_out, tokens_in, above, below, edge, mlp_gain, w_up, conv_kernel, w_down, w_out,
        w_query, w_key, w_value)
    hold = lax.optimization_barrier
    grad_row, row_tokens = hold((grad_row, row_tokens))
    grad_row = to_lines(grad_row.reshape(count_gx, rows // count_gx, cols, half), "gx")
    here = lax.axis_index("gy")
    col_send = cut_cols(grad_col, count_gy)
    col_parts = []
    for ahead in range(count_gy):
        part = lax.dynamic_index_in_dim(col_send, (here + ahead) % count_gy, 0, keepdims=False)
        if ahead:
            part = lax.ppermute(part, "gy", [(i, (i + ahead) % count_gy) for i in range(count_gy)])
        col_parts.append(part)
    col_at = (here - jnp.arange(count_gy, dtype=jnp.int32)) % count_gy
    row_out = attention((row_tokens, grad_row), col_at, (count_gx, rows // count_gx, cols), attn_gain, weights,
                        row_mask, 0)
    row_out, *col_parts = hold((row_out, *col_parts))
    row_back = to_lines(row_out, "gx").reshape(rows, cols, width)
    col_out = attention(tuple(col_parts), col_at, (count_gy, cols // count_gy, rows), attn_gain, weights,
                        col_mask, 1)
    row_back, col_out = hold((row_back, col_out))
    col_back = to_lines(col_out, "gy")
    return final(tokens_in, grad_mid, row_back, col_back, attn_gain)


def solution(mesh):
    tile = P("gy", "gx", None)
    return jax.shard_map(per_device, mesh=mesh, in_specs=(tile,) * 3 + (P(),) * 11, out_specs=tile, check_vma=False)
```

```python
import functools

import jax
import jax.numpy as jnp
from jax import lax
from jax.experimental import pallas as pl
from jax.experimental.pallas import tpu as pltpu
from jax.sharding import PartitionSpec as P

HEADS = 8
BLK = 128
EPSILON = 1e-05
GELU_C = 0.7978845608028654
LOG2E = 1.4426950408889634
LN2 = 0.6931471805599453
F32 = jnp.float32
BF16 = jnp.bfloat16
STRIDE = 64
GROUP = 8
CHUNK = GROUP * STRIDE
BIG = 8
FIN = 16
GUARD = 2
RING = 3 * GROUP
FC = 256


def dot_nt(a, b):
    return lax.dot_general(a, b, (((1,), (1,)), ((), ())), preferred_element_type=F32)


def gelu_slope(v):
    k = lambda x: jnp.asarray(x, v.dtype)
    u = v * v
    t = jnp.tanh(v * (k(GELU_C) + k(GELU_C * 0.044715) * u))
    poly = v * (k(0.5 * GELU_C) + k(1.5 * 0.044715 * GELU_C) * u)
    return (k(0.5) + k(0.5) * t) + (k(1.0) - t * t) * poly


def normalize(x):
    center = x - jnp.mean(x, axis=-1, keepdims=True)
    inv = lax.rsqrt(jnp.mean(center * center, axis=-1, keepdims=True) + EPSILON)
    return center * inv, inv


def mlp_kernel(rows, cols, mid_ref, gout_ref, tok_ref, above_ref, below_ref, edge_ref, gain_ref, wup_ref, conv_ref, wdown_ref, wout_ref,
               wq_ref, wk_ref, wv_ref,
               gm_ref, grow_ref, gcol_ref, wide_ref, x_s, y_s, wdt_s, wut_s, grad_s, *rings):
    width = mid_ref.shape[-1]
    gain = gain_ref[...]
    held = rows + 8
    trips = (rows + 4 + GROUP) // GROUP + 2
    tall = BIG * STRIDE

    def rows_at(row):
        return pl.multiple_of(row * STRIDE, STRIDE)

    edges = STRIDE - cols

    def place(ref, lead, row, values, count):
        for j in range(values.shape[0] // count):
            start = (row + j) * STRIDE + (0 if count == cols else cols)
            ref[lead + (pl.ds(pl.multiple_of(start, 16), count), slice(None))] = values[j * count:(j + 1) * count]

    def scaled(values):
        return normalize(values.astype(F32))[0] * gain

    none = jnp.zeros((cols, width), F32)
    for row in (0, 1, rows + 6, rows + 7, rows + 8, rows + 9):
        place(y_s, (0,), row, none, cols)
        place(grad_s, (), row, none.astype(BF16), cols)
    for ref, row in ((above_ref, 2), (below_ref, rows + 4)):
        values = ref[...].reshape(2 * cols, 2 * width)
        place(y_s, (0,), row, scaled(values[:, :width]), cols)
        place(grad_s, (), row, values[:, width:], cols)

    def edge_block(i, c):
        n = (rows + 10) // 2
        values = edge_ref[pl.ds(i * n, n)].reshape(n * edges, 2 * width)
        place(y_s, (0,), i * n, scaled(values[:, :width]), edges)
        place(grad_s, (), i * n, values[:, width:], edges)
        return c
    lax.fori_loop(0, 2, edge_block, 0)

    def norm_block(i, c):
        src = pl.ds(i * BIG, BIG)
        place(y_s, (0,), i * BIG + 4, scaled(mid_ref[src].reshape(BIG * cols, width)), cols)
        place(grad_s, (), i * BIG + 4, gout_ref[src].reshape(BIG * cols, width), cols)
        return c
    lax.fori_loop(0, rows // BIG, norm_block, 0)

    def shift_block(i, c):
        at = rows_at(i * BIG + 1)
        xv = y_s[0, pl.ds(at, tall + 8), :]
        lv = y_s[0, pl.ds(at - 8, tall + 8), :]
        dst = pl.ds(rows_at(i * BIG), tall)
        x_s[0, dst, :] = lv[7:7 + tall].astype(BF16)
        x_s[1, dst, :] = xv[:tall].astype(BF16)
        x_s[2, dst, :] = xv[1:1 + tall].astype(BF16)
        return c
    lax.fori_loop(0, held // BIG, shift_block, 0)

    n = width // 2
    for half in range(2):
        for j, ref in enumerate((wq_ref, wk_ref, wv_ref)):
            wide_ref[half, :, j * n:(j + 1) * n] = ref[:, half * n:(half + 1) * n]
    wdt_s[...] = wdown_ref[...].astype(F32).T.astype(BF16)
    wut_s[...] = wup_ref[...].astype(F32).T.astype(BF16)
    taps = [conv_ref[t:t + 1, :].astype(BF16) for t in range(9)]
    hidden = wup_ref.shape[1]
    parts_of = hidden // FC
    h_parts, gp_parts = rings[:parts_of], rings[parts_of:]

    def slot(row):
        return pl.ds(rows_at(lax.rem(row + 2 * RING, RING)), STRIDE)

    def products(i):
        z0 = GROUP * (i - 2) - 2
        for b in range(3):
            stack = []
            for part in range(parts_of):
                lanes = slice(part * FC, (part + 1) * FC)
                pile = []
                for sub in range(GROUP):
                    z = None
                    for a in range(3):
                        term = gp_parts[part][slot(z0 + 1 - a + sub), :] * taps[3 * a + b][:, lanes]
                        z = term if z is None else z + term
                    pile.append(z)
                stack.append(jnp.concatenate(pile, axis=0))
            y_s[b, pl.ds(rows_at(z0 + GUARD), CHUNK), :] = jnp.dot(
                jnp.concatenate(stack, axis=1), wut_s[...], preferred_element_type=F32)

    def slopes(i, part):
        g0 = GROUP * (i - 1) - 1
        h_s, gp_s = h_parts[part], gp_parts[part]
        grads = grad_s[pl.ds(rows_at(jnp.clip(g0 + 1, 0, held + 2 - GROUP)), CHUNK), :]
        lanes = slice(part * FC, (part + 1) * FC)
        ga = jnp.dot(grads, wdt_s[:, lanes], preferred_element_type=F32)
        for sub in range(GROUP):
            pre = None
            for a in range(3):
                for b in range(3):
                    term = h_s[b, slot(g0 + a - 1 + sub), :] * taps[3 * a + b][:, lanes]
                    pre = term if pre is None else pre + term
            gp_s[slot(g0 + sub), :] = (
                ga[sub * STRIDE:(sub + 1) * STRIDE] * gelu_slope(pre).astype(F32)).astype(BF16)

    def project(i, part):
        src = pl.ds(rows_at(jnp.minimum(GROUP * i, held - GROUP)), CHUNK)
        dst = pl.ds(rows_at(lax.rem(GROUP * i, RING)), CHUNK)
        lanes = slice(part * FC, (part + 1) * FC)
        for b in range(3):
            h_parts[part][b, dst, :] = jnp.dot(
                x_s[b, src, :], wup_ref[:, lanes], preferred_element_type=F32).astype(BF16)

    def body(i, c):
        products(i)
        for part in range(parts_of):
            slopes(i, part)
            project(i, part)
        return c

    for part in range(parts_of):
        project(0, part)
    for part in range(parts_of):
        slopes(1, part)
        project(1, part)
    lax.fori_loop(2, trips - 2, body, 0)
    products(trips - 2)
    for part in range(parts_of):
        slopes(trips - 2, part)
    products(trips - 1)

    deep = FIN * STRIDE

    def turned(values):
        return jnp.swapaxes(values.astype(F32).reshape(FIN, cols, values.shape[-1]), 0, 1).astype(BF16)

    def finish(i, c):
        base = rows_at(i * FIN + 3 + GUARD)
        right = y_s[0, pl.ds(base, deep + 8), :][1:1 + deep]
        left = y_s[2, pl.ds(base - 8, deep + 8), :][7:7 + deep]
        total = y_s[1, pl.ds(base, deep), :] + right + left

        def crop(v):
            return v.reshape(FIN, STRIDE, width)[:, :cols].reshape(FIN * cols, width)

        e = crop(total) * gain
        src = pl.ds(i * FIN, FIN)
        hat, inv = normalize(mid_ref[src].reshape(FIN * cols, width).astype(F32))
        res = gout_ref[src].reshape(FIN * cols, width).astype(F32) + inv * (
            e - jnp.mean(e, axis=-1, keepdims=True) - hat * jnp.mean(e * hat, axis=-1, keepdims=True))
        res = res.astype(BF16)
        dst = pl.ds(i * FIN, FIN)
        gm_ref[dst] = res.reshape(FIN, cols, width)
        ga = dot_nt(res, wout_ref[...])
        grow_ref[dst] = ga[:, :width // 2].astype(BF16).reshape(FIN, cols, width // 2)
        across = pl.ds(pl.multiple_of(i * FIN, FIN), FIN)
        gcol_ref[:, across, width:] = turned(ga[:, width // 2:])
        gcol_ref[:, across, :width] = turned(tok_ref[dst].astype(F32).reshape(FIN * cols, width))
        return c
    lax.fori_loop(0, rows // FIN, finish, 0)


def mlp(mid, grad, tokens, above, below, edge, gain, w_up, conv_kernel, w_down, w_out, w_query, w_key, w_value):
    rows, cols, width = mid.shape
    hidden = w_up.shape[1]
    held = rows + 8
    trips = (rows + 4 + GROUP) // GROUP + 2
    slots = max(GROUP * (trips - 2), rows + 12) * STRIDE
    whole = pl.BlockSpec(memory_space=pltpu.VMEM)
    return pl.pallas_call(
        functools.partial(mlp_kernel, rows, cols),
        out_shape=(
            jax.ShapeDtypeStruct((rows, cols, width), BF16), jax.ShapeDtypeStruct((rows, cols, width // 2), BF16),
            jax.ShapeDtypeStruct((cols, rows, width + width // 2), BF16),
            jax.ShapeDtypeStruct((2, width, 3 * width // 2), BF16),),
        in_specs=[whole] * 14,
        out_specs=(whole,) * 4,
        scratch_shapes=[
            pltpu.VMEM((3, held * STRIDE, width), BF16),
            pltpu.VMEM((3, slots, width), F32),
            pltpu.VMEM((width, hidden), BF16),
            pltpu.VMEM((hidden, width), BF16),
            pltpu.VMEM(((rows + 10) * STRIDE, width), BF16),
        ] + [pltpu.VMEM((3, RING * STRIDE, FC), BF16)] * (hidden // FC)
        + [pltpu.VMEM((RING * STRIDE, FC), BF16)] * (hidden // FC),
        compiler_params=pltpu.CompilerParams(vmem_limit_bytes=54 * 1024 * 1024),
        cost_estimate=pl.CostEstimate(flops=20_000_000_000, transcendentals=4_000_000, bytes_accessed=12_000_000),
        name="mlp_backward",
    )(mid, grad, tokens, above, below, edge, gain.reshape(1, -1), w_up, conv_kernel, w_down, w_out,
      w_query, w_key, w_value)


def attn_kernel(nl, nk, half, pieces, mask_ref, at_ref, *refs):
    x_ref, g_ref = refs[:2]
    piece_refs = refs[:pieces]
    (gain_ref, w_ref, out_ref, q_s, k_s, v_s, g_s, kt_s, qmt_s, qm_s, gmt_s, gm_s,
     e_s, dp_s, st_s, dq_s, dk_s, dv_s) = refs[max(pieces, 2):]
    heads = HEADS // 2
    hw = 128
    hd = hw // heads
    length = nk * BLK
    factor = hd ** -0.5
    gain = gain_ref[...]
    wide = heads * BLK

    qmt_s[...] = jnp.zeros_like(qmt_s)
    gmt_s[...] = jnp.zeros_like(gmt_s)
    dk_s[...] = jnp.zeros_like(dk_s)
    dv_s[...] = jnp.zeros_like(dv_s)

    def project(xv):
        normed = (normalize(xv.astype(F32))[0] * gain).astype(BF16)
        return jnp.dot(normed, w_ref[half], preferred_element_type=F32)

    def keep(line, where, qkv, grads):
        q_s[line, where, :] = (qkv[:, :hw] * (factor * LOG2E)).astype(BF16)
        k_s[line, where, :] = qkv[:, hw:2 * hw].astype(BF16)
        v_s[line, where, :] = qkv[:, 2 * hw:].astype(BF16)
        g_s[line, where, :] = grads

    if pieces:
        span = out_ref.shape[2]
        for piece, ref in enumerate(piece_refs):
            where = pl.ds(pl.multiple_of(at_ref[piece] * span, span), span)
            qkv = project(ref[:, :, :2 * hw].reshape(nl * span, 2 * hw))
            for line in range(nl):
                keep(line, where, qkv[line * span:(line + 1) * span], ref[line, :, 2 * hw:])
    else:
        def prepare(line, carry):
            keep(line, slice(None), project(x_ref[:, line].reshape(length, 2 * hw)),
                 g_ref[:, line].reshape(length, hw))
            return carry
        lax.fori_loop(0, nl, prepare, 0)

    def turn(line, carry):
        kt_s[line] = k_s[line].astype(F32).T.astype(BF16)
        return carry
    lax.fori_loop(0, nl, turn, 0)
    lane = lax.broadcasted_iota(jnp.int32, (BLK, hw), 1)

    def query_block(qb, carry):
        qs = pl.ds(pl.multiple_of(qb * BLK, BLK), BLK)
        for line in range(nl):
            for src, dt, dm in ((q_s, qmt_s, qm_s), (g_s, gmt_s, gm_s)):
                blk = src[line, qs, :]
                blk_f = blk.astype(F32)
                blk_t = blk_f.T.astype(BF16)
                for h in range(heads):
                    dt[line, h * hd:(h + 1) * hd, h * BLK:(h + 1) * BLK] = blk_t[h * hd:(h + 1) * hd]
                    inside = (lane >= h * hd) & (lane < (h + 1) * hd)
                    dm[line, h * BLK:(h + 1) * BLK, :] = jnp.where(inside, blk_f, 0.0).astype(BF16)

        def phase_a(kb, c):
            allowed = mask_ref[qb, kb] > 0
            ks = pl.ds(pl.multiple_of(kb * BLK, BLK), BLK)

            @pl.when(jnp.logical_not(allowed))
            def _():
                for line in range(nl):
                    st_s[kb, line] = jnp.concatenate(
                        [jnp.full((1, wide), -jnp.inf, F32), jnp.zeros((7, wide), F32)], axis=0)

            @pl.when(allowed)
            def _():
                for line in range(nl):
                    s = jnp.dot(k_s[line, ks, :], qmt_s[line], preferred_element_type=F32)
                    dp = jnp.dot(v_s[line, ks, :], gmt_s[line], preferred_element_type=F32)
                    top = jnp.max(s, axis=0, keepdims=True)
                    e = jnp.exp2(s - top)
                    e_s[kb, line] = e.astype(BF16)
                    dp_s[kb, line] = dp
                    st_s[kb, line, 0:1] = top
                    st_s[kb, line, 1:2] = jnp.sum(e, axis=0, keepdims=True)
                    st_s[kb, line, 2:3] = jnp.sum(e * dp, axis=0, keepdims=True)
            return c

        lax.fori_loop(0, nk, phase_a, 0)

        for line in range(nl):
            top = st_s[0, line, 0:1]
            for kb in range(1, nk):
                top = jnp.maximum(top, st_s[kb, line, 0:1])
            total = jnp.zeros((1, wide), F32)
            moment = jnp.zeros((1, wide), F32)
            weights = []
            for kb in range(nk):
                wk = jnp.exp2(st_s[kb, line, 0:1] - top)
                weights.append(wk)
                total = total + wk * st_s[kb, line, 1:2]
                moment = moment + wk * st_s[kb, line, 2:3]
            inv = 1.0 / total
            delta = moment * inv
            for kb in range(nk):
                st_s[kb, line, 3:4] = weights[kb] * inv
                st_s[kb, line, 4:5] = delta
            dq_s[line] = jnp.zeros((hd, wide), F32)

        def phase_b(kb, c):
            ks = pl.ds(pl.multiple_of(kb * BLK, BLK), BLK)

            @pl.when(mask_ref[qb, kb] > 0)
            def _():
                for line in range(nl):
                    p = e_s[kb, line].astype(F32) * st_s[kb, line, 3:4]
                    ds = (p * (dp_s[kb, line] - st_s[kb, line, 4:5])).astype(BF16)
                    dv_s[line, ks, :] += jnp.dot(p.astype(BF16), gm_s[line], preferred_element_type=F32)
                    dk_s[line, ks, :] += jnp.dot(ds, qm_s[line], preferred_element_type=F32)
                    for h in range(heads):
                        dq_s[line, :, h * BLK:(h + 1) * BLK] += jnp.dot(
                            kt_s[line, h * hd:(h + 1) * hd, ks], ds[:, h * BLK:(h + 1) * BLK],
                            preferred_element_type=F32)
            return c

        lax.fori_loop(0, nk, phase_b, 0)
        for line in range(nl):
            full = jnp.concatenate([dq_s[line, :, h * BLK:(h + 1) * BLK] for h in range(heads)], axis=0)
            q_s[line, qs, :] = (full.T * factor).astype(BF16)
        return carry

    lax.fori_loop(0, nk, query_block, 0)

    def finish(line, carry):
        grads = jnp.concatenate(
            [q_s[line], (dk_s[line] * LN2).astype(BF16), dv_s[line].astype(BF16)], axis=1)
        res = dot_nt(grads, w_ref[half]).astype(BF16)
        out_ref[:, line] = res.reshape(out_ref.shape[0], out_ref.shape[2], out_ref.shape[3])
        return carry

    lax.fori_loop(0, nl, finish, 0)


def attention(arrays, at, shape, gain, w_wide, mask, half):
    srcs, nl, span = shape
    pieces = srcs if len(arrays) == srcs else 0
    width = w_wide.shape[1]
    length = srcs * span
    nk = length // BLK
    hw = width // 2
    heads = HEADS // 2
    wide = heads * BLK
    vm = pl.BlockSpec(memory_space=pltpu.VMEM)
    pairs = nk * nk * nl
    return pl.pallas_call(
        functools.partial(attn_kernel, nl, nk, half, pieces),
        out_shape=jax.ShapeDtypeStruct((srcs, nl, span, width), BF16),
        in_specs=[pl.BlockSpec(memory_space=pltpu.SMEM)] * 2 + [vm] * (len(arrays) + 2),
        out_specs=vm,
        scratch_shapes=[
            pltpu.VMEM((nl, length, hw), BF16),
            pltpu.VMEM((nl, length, hw), BF16),
            pltpu.VMEM((nl, length, hw), BF16),
            pltpu.VMEM((nl, length, hw), BF16),
            pltpu.VMEM((nl, hw, length), BF16),
            pltpu.VMEM((nl, hw, wide), BF16),
            pltpu.VMEM((nl, wide, hw), BF16),
            pltpu.VMEM((nl, hw, wide), BF16),
            pltpu.VMEM((nl, wide, hw), BF16),
            pltpu.VMEM((nk, nl, BLK, wide), BF16),
            pltpu.VMEM((nk, nl, BLK, wide), F32),
            pltpu.VMEM((nk, nl, 8, wide), F32),
            pltpu.VMEM((nl, hw // heads, wide), F32),
            pltpu.VMEM((nl, length, hw), F32),
            pltpu.VMEM((nl, length, hw), F32),
        ],
        compiler_params=pltpu.CompilerParams(vmem_limit_bytes=28 * 1024 * 1024),
        cost_estimate=pl.CostEstimate(flops=pairs * 200_000_000, transcendentals=pairs * 65536, bytes_accessed=4_000_000),
        name="axial_attention",
    )(mask, at, *arrays, gain.reshape(1, -1), w_wide)


def final_kernel(tok_ref, mid_ref, row_ref, col_ref, gain_ref, out_ref):
    count, cols, width = tok_ref.shape

    def flat(ref):
        return ref[...].reshape(count * cols, width).astype(F32)

    hat, inv = normalize(flat(tok_ref))
    turned = jnp.swapaxes(col_ref[...].reshape(cols, count, width).astype(F32), 0, 1).reshape(count * cols, width)
    e = (flat(row_ref) + turned) * gain_ref[...]
    res = flat(mid_ref) + inv * (
        e - jnp.mean(e, axis=-1, keepdims=True) - hat * jnp.mean(e * hat, axis=-1, keepdims=True))
    out_ref[...] = res.astype(BF16).reshape(count, cols, width)


def final(tokens, grad_mid, row_back, col_back, gain):
    rows, cols, width = tokens.shape
    blk = pl.BlockSpec((16, cols, width), lambda i: (i, 0, 0))
    return pl.pallas_call(
        final_kernel,
        out_shape=jax.ShapeDtypeStruct(tokens.shape, BF16),
        grid=(rows // 16,),
        in_specs=[blk, blk, blk, pl.BlockSpec((*col_back.shape[:2], 16, width), lambda i: (0, 0, i, 0)), pl.BlockSpec((1, width), lambda i: (0, 0))],
        out_specs=blk,
        cost_estimate=pl.CostEstimate(flops=20_000_000, transcendentals=4_000, bytes_accessed=8_000_000),
        name="norm_backward",
    )(tokens, grad_mid, row_back, col_back, gain.reshape(1, -1))


def to_lines(blocks, axis):
    return lax.all_to_all(blocks, axis, split_axis=0, concat_axis=0, tiled=True)


def neighbours(ahead, behind, axis):
    count = lax.axis_size(axis)
    up = [(i, i + 1) for i in range(count - 1)]
    return lax.ppermute(ahead, axis, up), lax.ppermute(behind, axis, [(j, i) for i, j in up])


def per_device(tokens_in, saved_mid, grad_out, attn_gain, mlp_gain, w_query, w_key, w_value, w_out,
               w_up, conv_kernel, w_down, row_mask, col_mask):
    rows, cols, width = tokens_in.shape
    half = width // 2
    count_gx = lax.axis_size("gx")
    count_gy = lax.axis_size("gy")

    def both(rs, cs):
        return jnp.concatenate([saved_mid[rs, cs], grad_out[rs, cs]], axis=-1)

    every = slice(None)
    above, below = neighbours(both(slice(rows - 2, rows), every), both(slice(0, 2), every), "gy")
    row_tokens = to_lines(tokens_in.reshape(count_gx, rows // count_gx, cols, width), "gx")
    sides = [jnp.concatenate([above[:, cs], both(every, cs), below[:, cs]], axis=0)
             for cs in (slice(cols - 2, cols), slice(0, 2))]
    left, right = neighbours(sides[0], sides[1], "gx")
    edge = jnp.concatenate([
        jnp.pad(right, ((2, 4), (0, 0), (0, 0))),
        jnp.zeros((rows + 10, STRIDE - cols - 4, 2 * width), BF16),
        jnp.pad(left, ((1, 5), (0, 0), (0, 0)))], axis=1)
    grad_mid, grad_row, grad_col, weights = mlp(
        saved_mid, grad_out, tokens_in, above, below, edge, mlp_gain, w_up, conv_kernel, w_down, w_out,
        w_query, w_key, w_value)
    hold = lax.optimization_barrier
    grad_row, row_tokens = hold((grad_row, row_tokens))
    grad_row = to_lines(grad_row.reshape(count_gx, rows // count_gx, cols, half), "gx")
    here = lax.axis_index("gy")
    col_send = grad_col.reshape(count_gy, cols // count_gy, rows, grad_col.shape[-1])
    col_parts = []
    for ahead in range(count_gy):
        part = lax.dynamic_index_in_dim(col_send, (here + ahead) % count_gy, 0, keepdims=False)
        if ahead:
            part = lax.ppermute(part, "gy", [(i, (i + ahead) % count_gy) for i in range(count_gy)])
        col_parts.append(part)
    col_at = (here - jnp.arange(count_gy, dtype=jnp.int32)) % count_gy
    row_out = attention((row_tokens, grad_row), col_at, (count_gx, rows // count_gx, cols), attn_gain, weights,
                        row_mask, 0)
    row_out, *col_parts = hold((row_out, *col_parts))
    row_back = to_lines(row_out, "gx").reshape(rows, cols, width)
    col_out = attention(tuple(col_parts), col_at, (count_gy, cols // count_gy, rows), attn_gain, weights,
                        col_mask, 1)
    row_back, col_out = hold((row_back, col_out))
    col_back = to_lines(col_out, "gy")
    return final(tokens_in, grad_mid, row_back, col_back, attn_gain)


def solution(mesh):
    tile = P("gy", "gx", None)
    return jax.shard_map(per_device, mesh=mesh, in_specs=(tile,) * 3 + (P(),) * 11, out_specs=tile, check_vma=False)
```
